32 devices in a mesh: gx: 4 (over z), gy: 2 (over x), gz: 4 (over y, core).
Axes of the slice: x: 2, y: 2, z: 4, core: 2. Of those that a mesh axis runs over, the one named last changes fastest.
Arguments:
- charges: float32 [32, 2, 4, 512], P('gx', 'gy', 'gz'), may hold values from -3 to 3
- offsets: float32 [3, 32, 2, 4, 512], P(None, 'gx', 'gy', 'gz'), may hold values from 0 to 1
- cells: int32 [2, 32, 2, 4, 512], P(None, 'gx', 'gy', 'gz'), may hold values from 0 to 511, as said below
- kernel: bfloat16 [17, 17, 17], replicated, may hold values from -0.078125 to 0.078125
Outputs:
- potential: float32 [32, 16, 512], P('gx', 'gy', 'gz')
- forces: float32 [3, 32, 2, 4, 512], P(None, 'gx', 'gy', 'gz')
The draws below stay inside these ranges and needn't reach their ends.
Inputs may be any that keep to these rules, and one draw needn't show every extreme that they name: cells[0] lies in the block of 8 rows that belongs to the atom's second index (index g: g * 8 to g * 8 + 7); cells[1] lies likewise in the block of 128 that belongs to its third index.
All inputs are finite; a program needn't handle non-finite values.
Results may differ from the reference program's by a relative error of at most 0.0029.
Values may be sent and summed in bfloat16 or wider, within the bound.
No kernel may reach another device: no remote copies, remote signals or barrier semaphores. Data moves between devices by JAX's collectives and lax.ppermute only.
A program may use at most 64 MiB of HBM per device.

```python
import jax
import jax.numpy as jnp
from jax import lax

CY = 8
CZ = 128
APT = 512
KSPAN = 17
NX = 32
NY = 16
NZ = 512
N_GY = 2
N_GZ = 4


def draw_cells(key, part):
    key_y, key_z = jax.random.split(jax.random.fold_in(key, 17))
    array_shape = (NX, NY // CY, NZ // CZ, APT)
    local_y = jax.random.randint(key_y, array_shape, 0, CY, dtype=jnp.int32)
    local_z = jax.random.randint(key_z, array_shape, 0, CZ, dtype=jnp.int32)
    block_y = jnp.arange(NY // CY, dtype=jnp.int32)[None, :, None, None] * CY
    block_z = jnp.arange(NZ // CZ, dtype=jnp.int32)[None, None, :, None] * CZ
    return jnp.stack([local_y + block_y, local_z + block_z]).astype(jnp.int32)


def block_levels(stream_key, shape, shards, low, top_value):
    def one(dim, parts):
        draws = jax.random.uniform(jax.random.fold_in(jax.random.fold_in(stream_key, 6), dim), (parts,), jnp.float32, low / len(shards), top_value / len(shards))
        return jnp.repeat(jnp.exp(draws), shape[dim] // parts).reshape((-1,) + (1,) * (len(shape) - dim - 1))

    level = one(*shards[0])
    for cut in shards[1:]:
        level = level * one(*cut)
    return level


def normal_values(key, extent, deviation, bound, cuts=(), kind=jnp.bfloat16):
    result = deviation * jax.random.normal(key, extent, jnp.float32)
    if cuts:
        result = result * block_levels(key, extent, cuts, -0.22, 0.18)
    return jnp.clip(result, -bound, bound).astype(kind)


def setup_inputs(seed: int = 0) -> dict:
    arg_keys = jax.random.split(jax.random.key(seed), 5)
    return {
        "charges": normal_values(arg_keys[0], (NX, N_GY, N_GZ, APT), 0.5, 3.0, ((0, 4), (1, 2), (2, 4)), jnp.float32),
        "offsets": jnp.clip(1.0 * jax.random.uniform(arg_keys[1], (3, NX, N_GY, N_GZ, APT), jnp.float32) ** block_levels(arg_keys[1], (3, NX, N_GY, N_GZ, APT), ((1, 4), (2, 2), (3, 4)), -0.2, 0.2), 0.0, 1.0),
        "cells": draw_cells(jax.random.fold_in(arg_keys[4], 71), 0),
        "kernel": normal_values(arg_keys[3], (KSPAN, KSPAN, KSPAN), (KSPAN * KSPAN * KSPAN) ** -0.5, 0.078125),
    }


def spline(fraction):
    remain = 1.0 - fraction
    values = [remain ** 3 / 6.0,
              (3.0 * fraction ** 3 - 6.0 * fraction ** 2 + 4.0) / 6.0,
              (-3.0 * fraction ** 3 + 3.0 * fraction ** 2 + 3.0 * fraction + 1.0) / 6.0,
              fraction ** 3 / 6.0]
    slopes = [-0.5 * remain ** 2,
              1.5 * fraction ** 2 - 2.0 * fraction,
              -1.5 * fraction ** 2 + fraction + 0.5,
              0.5 * fraction ** 2]
    return values, slopes


def reference(charges, offsets, cells, kernel):
    plane = jnp.broadcast_to(jnp.arange(NX, dtype=jnp.int32)[:, None, None, None], charges.shape).reshape(-1)
    column_y = cells[0].reshape(-1)
    column_z = cells[1].reshape(-1)
    charge_flat = charges.reshape(-1)
    x_values, x_slopes = spline(offsets[0].reshape(-1))
    y_values, y_slopes = spline(offsets[1].reshape(-1))
    z_values, z_slopes = spline(offsets[2].reshape(-1))
    grid = jnp.zeros((NX * NY * NZ,), jnp.float32)
    for shift_a in range(4):
        for shift_b in range(4):
            row_index = ((plane + shift_a - 1) % NX) * NY + (column_y + shift_b - 1) % NY
            weight_ab = charge_flat * x_values[shift_a] * y_values[shift_b]
            for shift_c in range(4):
                target = (row_index * NZ + (column_z + shift_c - 1) % NZ).astype(jnp.int32)
                grid = grid.at[target].add(weight_ab * z_values[shift_c])
    rounded = lax.optimization_barrier(grid.reshape(NX, NY, NZ).astype(jnp.bfloat16)).astype(jnp.float32)
    radius = KSPAN // 2
    spots = radius - jnp.arange(KSPAN, dtype=jnp.int32)
    wrapped = jnp.zeros((NX, NY, NZ), jnp.float32).at[
        (spots % NX)[:, None, None], (spots % NY)[None, :, None], (spots % NZ)[None, None, :]
    ].add(kernel.astype(jnp.float32))
    potential = jnp.fft.irfftn(jnp.fft.rfftn(rounded) * jnp.fft.rfftn(wrapped), s=(NX, NY, NZ)).astype(jnp.float32)
    flat_potential = potential.reshape(-1)
    force_x = jnp.zeros_like(charge_flat)
    force_y = jnp.zeros_like(charge_flat)
    force_z = jnp.zeros_like(charge_flat)
    for shift_a in range(4):
        for shift_b in range(4):
            row_index = ((plane + shift_a - 1) % NX) * NY + (column_y + shift_b - 1) % NY
            for shift_c in range(4):
                target = (row_index * NZ + (column_z + shift_c - 1) % NZ).astype(jnp.int32)
                sample = flat_potential[target]
                force_x = force_x + x_slopes[shift_a] * y_values[shift_b] * z_values[shift_c] * sample
                force_y = force_y + x_values[shift_a] * y_slopes[shift_b] * z_values[shift_c] * sample
                force_z = force_z + x_values[shift_a] * y_values[shift_b] * z_slopes[shift_c] * sample
    forces = -charge_flat[None, :] * jnp.stack([force_x, force_y, force_z])
    return potential, forces.reshape(3, NX, N_GY, N_GZ, APT)
```

```python
import functools

import jax
import jax.numpy as jnp
from jax import lax
from jax.experimental import pallas as pl
from jax.experimental.pallas import tpu as pltpu
from jax.sharding import PartitionSpec as P

CY = 8
CZ = 128
EXT = 3
ROWS = 16
LANES = 32
GROUPS = 128 // LANES

F32 = jnp.float32
BF16 = jnp.bfloat16


def spline(fraction):
    remain = 1.0 - fraction
    values = [
        remain**3 / 6.0,
        (3.0 * fraction**3 - 6.0 * fraction**2 + 4.0) / 6.0,
        (-3.0 * fraction**3 + 3.0 * fraction**2 + 3.0 * fraction + 1.0) / 6.0,
        fraction**3 / 6.0,
    ]
    slopes = [
        -0.5 * remain**2,
        1.5 * fraction**2 - 2.0 * fraction,
        -1.5 * fraction**2 + fraction + 0.5,
        0.5 * fraction**2,
    ]
    return values, slopes


def pick(distance, four):
    out = jnp.zeros((), F32)
    for c in reversed(range(4)):
        out = jnp.where(distance == c, four[c], out)
    return out


def split(x):
    high = x.astype(BF16)
    return high, (x - high.astype(F32)).astype(BF16)


def nt_dot(a, b):
    return lax.dot_general(a, b, (((1,), (1,)), ((), ())), preferred_element_type=F32)


def iota(shape, dim):
    return lax.broadcasted_iota(jnp.int32, shape, dim)


def spread_kernel(tiles, chunks, group_planes, charge_ref, offset_ref, cell_ref, main_ref, z0_ref, z1_ref, acc):
    rows_total = tiles * chunks
    acc[...] = jnp.zeros_like(acc)
    row = iota((CZ + 2 * LANES, 128), 0)
    lower = row - CZ
    upper = row - CZ - LANES
    z_of_row = jnp.where(
        row < CZ,
        row,
        jnp.where(
            lower < LANES,
            jnp.where(lower < LANES // 2, lower, lower - LANES),
            jnp.where(upper < LANES // 2, CZ + upper, CZ - LANES + upper),
        ),
    )
    y_row = iota((ROWS, 128), 0)
    y_of_row = jnp.where(y_row < 12, y_row, y_row - ROWS)
    for t in range(tiles):
        s_high, s_low, z_high, z_low = [], [], [], []
        for j in range(chunks):
            r = t * chunks + j
            charge = charge_ref[pl.ds(r, 1), :]
            xv, _ = spline(offset_ref[pl.ds(r, 1), :])
            yv, _ = spline(offset_ref[pl.ds(rows_total + r, 1), :])
            zv, _ = spline(offset_ref[pl.ds(2 * rows_total + r, 1), :])
            cy = cell_ref[pl.ds(r, 1), :] & (CY - 1)
            cz = cell_ref[pl.ds(rows_total + r, 1), :] & (CZ - 1)
            y_dense = pick(y_of_row - (cy - 1), yv)
            z_dense = pick(z_of_row - (cz - 1), zv)
            s = jnp.concatenate([y_dense * (charge * xv[k]) for k in range(4)], 0)
            high, low = split(s)
            s_high.append(high)
            s_low.append(low)
            high, low = split(z_dense)
            z_high.append(high)
            z_low.append(low)
        s_high = jnp.concatenate(s_high, 1)
        s_low = jnp.concatenate(s_low, 1)
        z_high = jnp.concatenate(z_high, 1)
        z_low = jnp.concatenate(z_low, 1)
        both = nt_dot(jnp.concatenate([s_high, s_low], 0), z_high)
        got = both[: 4 * ROWS] + both[4 * ROWS :] + nt_dot(s_high, z_low)
        acc[t * ROWS : (t + 4) * ROWS, : CZ + 2 * LANES] += got
    planes = tiles + EXT
    main_ref[...] = acc[: planes * ROWS, :CZ]
    group = group_planes * ROWS
    lane = iota((group, 128), 1)
    lower_out = jnp.zeros((group, 128), F32)
    upper_out = jnp.zeros((group, 128), F32)
    for g in range(GROUPS):
        edge = acc[g * group : (g + 1) * group, CZ : CZ + 128]
        low = jnp.where(lane < LANES, edge, 0.0)
        high = jnp.where((lane >= LANES) & (lane < 2 * LANES), edge, 0.0)
        lower_out = lower_out + (pltpu.roll(low, g * LANES, 1) if g else low)
        upper_out = upper_out + pltpu.roll(high, (g * LANES - LANES) % 128, 1)
    even = lax.rem(lax.axis_index("gz"), 2) == 0
    z0_ref[...] = jnp.where(even, upper_out, lower_out)
    z1_ref[...] = jnp.where(even, lower_out, upper_out)


def z_fold_kernel(tiles, group_planes, main_ref, z0_ref, z1_ref, got0_ref, got1_ref, out_ref):
    planes = tiles + EXT
    group = group_planes * ROWS
    even = lax.rem(lax.axis_index("gz"), 2) == 0
    z0, z1, got0, got1 = z0_ref[...], z1_ref[...], got0_ref[...], got1_ref[...]
    own_upper = jnp.where(even, z0, z1)
    own_lower = jnp.where(even, z1, z0)
    right_lower = jnp.where(even, got0, got1)
    left_upper = jnp.where(even, got1, got0)
    lane = iota((group, 128), 1)
    first = (lane & (LANES - 1)) < LANES // 2
    halo = jnp.where(first, right_lower + own_upper, left_upper + own_lower)
    inner = jnp.where(first, left_upper, right_lower)
    for g in range(GROUPS):
        count = min(group, planes * ROWS - g * group)
        low = pltpu.roll(inner, (-g * LANES) % 128, 1) if g else inner
        high = pltpu.roll(inner, (128 - LANES - g * LANES) % 128, 1)
        add = jnp.where(lane < LANES // 2, low, jnp.where(lane >= 128 - LANES // 2, high, 0.0))
        out_ref[g * group : g * group + count, :] = (
            main_ref[g * group : g * group + count, :] + add[:count]
        )
    out_ref[planes * ROWS : planes * ROWS + group, :] = halo


def y_fold_kernel(n_gy, units, tiles, group_planes, *refs):
    sources, (out_ref, far_ref) = refs[:n_gy], refs[n_gy:]
    half = iota((CY, 128), 0) < CY // 2
    wide = n_gy * CY
    planes = tiles + EXT
    for u in range(units):
        blocks = [None] * n_gy

        def add(b, value):
            b = b % n_gy
            blocks[b] = value if blocks[b] is None else blocks[b] + value

        for b, ref in enumerate(sources):
            add(b, ref[u * ROWS : u * ROWS + CY, :])
            rest = ref[u * ROWS + CY : (u + 1) * ROWS, :]
            if n_gy == 2:
                add(b + 1, rest)
            else:
                add(b + 1, jnp.where(half, rest, 0.0))
                add(b - 1, jnp.where(half, 0.0, rest))
        value = jnp.concatenate(blocks, 0).astype(BF16)
        out_ref[u * wide : (u + 1) * wide, :] = value
        if u < EXT:
            far_ref[u * wide : (u + 1) * wide, :] = value
        elif planes - EXT <= u:
            v = u - (planes - EXT) + EXT
            far_ref[v * wide : (v + 1) * wide, :] = value


def field_kernel(
    tiles, chunks, group_planes, wide, span,
    own_ref, got1_ref, got3_ref, lower_ref, upper_ref, band_ref,
    charge_ref, offset_ref, cell_ref, potential_ref, force_ref, window, samples,
):
    planes = tiles + EXT
    radius = span // 2
    even = lax.rem(lax.axis_index("gx"), 2) == 0
    got1, got3 = got1_ref[...], got3_ref[...]
    right = jnp.where(even, got1, got3)
    left = jnp.where(even, got3, got1)
    own = own_ref[...]
    lane = iota((wide, 128), 1)
    margin = planes * wide

    def main(block, p):
        return block[p * wide : (p + 1) * wide].astype(F32)

    def edge(block, p, base=margin):
        g, q = divmod(p, group_planes)
        packed = block[base + q * wide : base + (q + 1) * wide].astype(F32)
        low = pltpu.roll(packed, (-g * LANES) % 128, 1) if g else packed
        high = pltpu.roll(packed, (128 - LANES - g * LANES) % 128, 1)
        return jnp.where(lane < LANES // 2, low, jnp.where(lane >= 128 - LANES // 2, high, 0.0))

    far_low, far_high = lower_ref[...], upper_ref[...]
    far_base = 2 * EXT * wide
    for x in range(2 * radius + planes):
        terms = []
        if x < planes:
            terms.append((main(left, x), edge(left, x)))
        if 0 <= x - tiles < planes:
            terms.append((main(own, x - tiles), edge(own, x - tiles)))
        if 0 <= x - 2 * tiles < planes:
            terms.append((main(right, x - 2 * tiles), edge(right, x - 2 * tiles)))
        if x < EXT:
            terms.append((main(far_low, EXT + x), edge(far_low, planes - EXT + x, far_base)))
        if 0 <= x - 3 * tiles < EXT:
            terms.append((main(far_high, x - 3 * tiles), edge(far_high, x - 3 * tiles, far_base)))
        window[x * wide : (x + 1) * wide, :128] = sum(a for a, _ in terms).astype(BF16)
        window[x * wide : (x + 1) * wide, 128:] = sum(b for _, b in terms).astype(BF16)

    band = band_ref[...]
    for x in range(planes):
        part = jnp.dot(
            band, window[x * wide : (x + span) * wide, :], preferred_element_type=F32
        )
        total = part[radius * ROWS : (radius + 1) * ROWS]
        for k in range(span):
            if k != radius:
                total = total + pltpu.roll(part[k * ROWS : (k + 1) * ROWS], (radius - k) % 256, 1)
        if 1 <= x <= tiles:
            potential_ref[x - 1] = total[:CY, :CZ]
        for c in range(4):
            moved = total if c == 1 else pltpu.roll(total, (1 - c) % 256, 1)
            samples[c, x * ROWS : (x + 1) * ROWS, :] = moved[:, :128]

    rows_total = tiles * chunks
    per = 8 // chunks
    upper_half = [iota((8, 128), 0) >= chunks * h for h in range(per)]
    for pair in range(tiles // per):
        rows = pl.ds(pair * 8, 8)
        charge = charge_ref[rows, :]
        xv, xs = spline(offset_ref[pl.ds(pair * 8, 8), :])
        yv, ys = spline(offset_ref[pl.ds(rows_total + pair * 8, 8), :])
        zv, zs = spline(offset_ref[pl.ds(2 * rows_total + pair * 8, 8), :])
        cy = cell_ref[pl.ds(pair * 8, 8), :] & (CY - 1)
        cz = cell_ref[pl.ds(rows_total + pair * 8, 8), :] & (CZ - 1)
        plain = [jnp.zeros((8, 128), F32) for _ in range(4)]
        along_y = [jnp.zeros((8, 128), F32) for _ in range(4)]
        along_z = [jnp.zeros((8, 128), F32) for _ in range(4)]
        for y in range(-1, CY + 2):
            distance = y + 1 - cy
            y_value = pick(distance, yv)
            y_slope = pick(distance, ys)
            row = y % ROWS
            for k in range(4):
                value = jnp.zeros((8, 128), F32)
                slope = jnp.zeros((8, 128), F32)
                for c in range(4):
                    source = None
                    for h in range(per):
                        at = (pair * per + h + k) * ROWS + row
                        line = jnp.broadcast_to(samples[c, at : at + 1, :], (8, 128))
                        source = line if h == 0 else jnp.where(upper_half[h], line, source)
                    picked = jnp.take_along_axis(source, cz, axis=1)
                    value = value + zv[c] * picked
                    slope = slope + zs[c] * picked
                plain[k] = plain[k] + y_value * value
                along_y[k] = along_y[k] + y_slope * value
                along_z[k] = along_z[k] + y_value * slope
        force_ref[0, rows, :] = -charge * sum(xs[k] * plain[k] for k in range(4))
        force_ref[1, rows, :] = -charge * sum(xv[k] * along_y[k] for k in range(4))
        force_ref[2, rows, :] = -charge * sum(xv[k] * along_z[k] for k in range(4))


def band_matrix(kernel, wide):
    span = kernel.shape[0]
    radius = span // 2
    row = jnp.arange(ROWS, dtype=jnp.int32)
    y_of_row = jnp.where(row < 12, row, row - ROWS)
    column = jnp.arange(wide, dtype=jnp.int32)
    tap = jnp.arange(span, dtype=jnp.int32)
    gap = column[None, None, :] - y_of_row[None, :, None] + radius - tap[:, None, None]
    chosen = (jnp.remainder(gap, wide) == 0).astype(BF16)
    band = jnp.einsum("ijk,jry->kriy", kernel, chosen, preferred_element_type=F32)
    return band.astype(BF16).reshape(span * ROWS, span * wide)


def vmem(n):
    return [pl.BlockSpec(memory_space=pltpu.VMEM)] * n


def local(charges, offsets, cells, kernel):
    n_gx, n_gy, n_gz = (lax.axis_size(axis) for axis in ("gx", "gy", "gz"))
    tiles, slots = charges.shape[0], charges.shape[3]
    span = kernel.shape[0]
    chunks = slots // 128
    rows = tiles * chunks
    planes = tiles + EXT
    group_planes = -(-planes // GROUPS)
    group = group_planes * ROWS
    wide = n_gy * CY
    charge = charges.reshape(rows, 128)
    offset = offsets.reshape(3 * rows, 128)
    cell = cells.reshape(2 * rows, 128)

    def shape(*dims, kind=F32):
        return jax.ShapeDtypeStruct(dims, kind)

    near = lambda n: [(i, i ^ 1) for i in range(n)]
    other = lambda n: [(i, (i + 1 if i % 2 else i - 1) % n) for i in range(n)]
    shift = lambda n, s: [(i, (i + s) % n) for i in range(n)]

    main, z0, z1 = pl.pallas_call(
        functools.partial(spread_kernel, tiles, chunks, group_planes),
        out_shape=(shape(planes * ROWS, 128), shape(group, 128), shape(group, 128)),
        in_specs=vmem(3),
        out_specs=tuple(vmem(3)),
        scratch_shapes=[pltpu.VMEM((GROUPS * group, CZ + 128), F32)],
        name="spread",
    )(charge, offset, cell)
    got0 = lax.ppermute(z0, "gz", near(n_gz))
    got1 = lax.ppermute(z1, "gz", other(n_gz))
    units = planes + group_planes
    block = pl.pallas_call(
        functools.partial(z_fold_kernel, tiles, group_planes),
        out_shape=shape(units * ROWS, 128),
        in_specs=vmem(5),
        out_specs=vmem(1)[0],
        name="z_fold",
    )(main, z0, z1, got0, got1)
    sources = [block] + [lax.ppermute(block, "gy", shift(n_gy, -s)) for s in range(1, n_gy)]
    mine, far = pl.pallas_call(
        functools.partial(y_fold_kernel, n_gy, units, tiles, group_planes),
        out_shape=(shape(units * wide, 128, kind=BF16), shape((2 * EXT + group_planes) * wide, 128, kind=BF16)),
        in_specs=vmem(n_gy),
        out_specs=tuple(vmem(2)),
        name="y_fold",
    )(*sources)
    x1 = lax.ppermute(mine, "gx", near(n_gx))
    if n_gx == 4:
        lower = upper = lax.ppermute(far, "gx", shift(n_gx, 2))
    else:
        lower = lax.ppermute(far, "gx", shift(n_gx, 2))
        upper = lax.ppermute(far, "gx", shift(n_gx, -2))
    x3 = lax.ppermute(mine, "gx", other(n_gx))
    band = band_matrix(kernel, wide)
    potential, forces = pl.pallas_call(
        functools.partial(field_kernel, tiles, chunks, group_planes, wide, span),
        out_shape=(shape(tiles, CY, CZ), shape(3, rows, 128)),
        in_specs=vmem(9),
        out_specs=tuple(vmem(2)),
        scratch_shapes=[
            pltpu.VMEM(((2 * (span // 2) + planes) * wide, 256), BF16),
            pltpu.VMEM((4, planes * ROWS, 128), F32),
        ],
        name="field",
    )(mine, x1, x3, lower, upper, band, charge, offset, cell)
    return potential, forces.reshape(3, tiles, 1, 1, slots)


def solution(mesh):
    placed = (
        P("gx", "gy", "gz", None),
        P(None, "gx", "gy", "gz", None),
        P(None, "gx", "gy", "gz", None),
        P(),
    )
    return jax.shard_map(
        local,
        mesh=mesh,
        in_specs=placed,
        out_specs=(P("gx", "gy", "gz"), P(None, "gx", "gy", "gz", None)),
        check_vma=False,
    )
```

```python
import functools

import jax
import jax.numpy as jnp
from jax import lax
from jax.experimental import pallas as pl
from jax.experimental.pallas import tpu as pltpu
from jax.sharding import PartitionSpec as P

CY = 8
CZ = 128
EXT = 3
ROWS = 16
LANES = 32
GROUPS = 128 // LANES

F32 = jnp.float32
BF16 = jnp.bfloat16


def spline(fraction):
    remain = 1.0 - fraction
    values = [
        remain**3 / 6.0,
        (3.0 * fraction**3 - 6.0 * fraction**2 + 4.0) / 6.0,
        (-3.0 * fraction**3 + 3.0 * fraction**2 + 3.0 * fraction + 1.0) / 6.0,
        fraction**3 / 6.0,
    ]
    slopes = [
        -0.5 * remain**2,
        1.5 * fraction**2 - 2.0 * fraction,
        -1.5 * fraction**2 + fraction + 0.5,
        0.5 * fraction**2,
    ]
    return values, slopes


def pick(distance, four):
    out = jnp.zeros((), F32)
    for c in reversed(range(4)):
        out = jnp.where(distance == c, four[c], out)
    return out


def split(x):
    high = x.astype(BF16)
    return high, (x - high.astype(F32)).astype(BF16)


def nt_dot(a, b):
    return lax.dot_general(a, b, (((1,), (1,)), ((), ())), preferred_element_type=F32)


def iota(shape, dim, kind=jnp.int32):
    return lax.broadcasted_iota(kind, shape, dim)


def tall(row, kind, count):
    tile = jnp.broadcast_to(row, (16, 128)).astype(kind)
    return jnp.concatenate([tile] * (count // 16), 0)


def z_weights(z_of_row, cell, rows):
    count = z_of_row.shape[0]
    high = low = jnp.zeros((count, 128), BF16)
    for c in range(4):
        here = z_of_row == tall(cell + (c - 1), jnp.int16, count)
        high = jnp.where(here, tall(rows[c], BF16, count), high)
        low = jnp.where(here, tall(rows[4 + c], BF16, count), low)
    return high, low


def edge_kernel(
    tiles, chunks, group_planes, charge_hbm, offset_hbm, cell_hbm,
    z0_ref, z1_ref, high_ref, low_ref, weight_ref, cell_ref,
    charge_in, offset_in, cell_in, x_rows, y_rows, acc, sems,
):
    copies = [
        pltpu.make_async_copy(source, target, sems.at[n])
        for n, (source, target) in enumerate(
            ((charge_hbm, charge_in), (offset_hbm, offset_in), (cell_hbm, cell_in))
        )
    ]
    for copy in copies:
        copy.start()
    rows = tiles * chunks
    acc[...] = jnp.zeros_like(acc)
    row = iota((2 * LANES, 128), 0, jnp.int16)
    upper = row - LANES
    z_of_row = jnp.where(
        row < LANES,
        jnp.where(row < LANES // 2, row, row - LANES),
        jnp.where(upper < LANES // 2, CZ + upper, CZ - LANES + upper),
    )
    y_row = iota((ROWS, 128), 0)
    y_of_row = jnp.where(y_row < 12, y_row, y_row - ROWS)
    for copy in copies:
        copy.wait()
    for r in range(0, rows, 8):
        at = pl.ds(r, 8)
        xv, _ = spline(offset_in[at, :])
        yv, _ = spline(offset_in[pl.ds(rows + r, 8), :])
        zv, _ = spline(offset_in[pl.ds(2 * rows + r, 8), :])
        charge = charge_in[at, :]
        for c in range(4):
            x_rows[c, at, :] = charge * xv[c]
            y_rows[c, at, :] = yv[c]
            high = zv[c].astype(BF16).astype(F32)
            weight_ref[c, at, :] = high
            weight_ref[4 + c, at, :] = zv[c] - high
        cell_ref[at, :] = cell_in[pl.ds(rows + r, 8), :] & (CZ - 1)
    for t in range(tiles):
        parts = [], [], [], []
        for j in range(chunks):
            at = pl.ds(t * chunks + j, 1)
            cy = cell_in[at, :] & (CY - 1)
            y_dense = pick(y_of_row - (cy - 1), [y_rows[c, at, :] for c in range(4)])
            s = jnp.concatenate([y_dense * x_rows[k, at, :] for k in range(4)], 0)
            z = z_weights(z_of_row, cell_ref[at, :], [weight_ref[c, at, :] for c in range(8)])
            for part, value in zip(parts, split(s) + z):
                part.append(value)
        s_high, s_low, z_high, z_low = (jnp.concatenate(part, 1) for part in parts)
        high_ref[t * 4 * ROWS : (t + 1) * 4 * ROWS, :] = s_high
        low_ref[t * 4 * ROWS : (t + 1) * 4 * ROWS, :] = s_low
        both = nt_dot(jnp.concatenate([s_high, s_low], 0), z_high)
        got = both[: 4 * ROWS] + both[4 * ROWS :] + nt_dot(s_high, z_low)
        acc[t * ROWS : (t + 4) * ROWS, : 2 * LANES] += got
    group = group_planes * ROWS
    lane = iota((group, 128), 1)
    lower_out = jnp.zeros((group, 128), F32)
    upper_out = jnp.zeros((group, 128), F32)
    for g in range(GROUPS):
        edge = acc[g * group : (g + 1) * group, :]
        low = jnp.where(lane < LANES, edge, 0.0)
        high = jnp.where(lane >= LANES, edge, 0.0)
        lower_out = lower_out + (pltpu.roll(low, g * LANES, 1) if g else low)
        upper_out = upper_out + pltpu.roll(high, (g * LANES - LANES) % 128, 1)
    even = lax.rem(lax.axis_index("gz"), 2) == 0
    z0_ref[...] = jnp.where(even, upper_out, lower_out)
    z1_ref[...] = jnp.where(even, lower_out, upper_out)


def spread_kernel(tiles, chunks, high_ref, low_ref, weight_ref, cell_ref, main_ref):
    main_ref[...] = jnp.zeros_like(main_ref)
    z_of_row = iota((CZ, 128), 0, jnp.int16)
    for t in range(tiles):
        parts = [], []
        for j in range(chunks):
            at = pl.ds(t * chunks + j, 1)
            z = z_weights(z_of_row, cell_ref[at, :], [weight_ref[c, at, :] for c in range(8)])
            for part, value in zip(parts, z):
                part.append(value)
        z_high, z_low = (jnp.concatenate(part, 1) for part in parts)
        s_high = high_ref[t * 4 * ROWS : (t + 1) * 4 * ROWS, :]
        s_low = low_ref[t * 4 * ROWS : (t + 1) * 4 * ROWS, :]
        both = nt_dot(jnp.concatenate([s_high, s_low], 0), z_high)
        got = both[: 4 * ROWS] + both[4 * ROWS :] + nt_dot(s_high, z_low)
        main_ref[t * ROWS : (t + 4) * ROWS, :] += got


def z_fold_kernel(tiles, group_planes, main_ref, z0_ref, z1_ref, got0_ref, got1_ref, out_ref, sent_ref):
    planes = tiles + EXT
    group = group_planes * ROWS
    even = lax.rem(lax.axis_index("gz"), 2) == 0
    z0, z1, got0, got1 = z0_ref[...], z1_ref[...], got0_ref[...], got1_ref[...]
    own_upper = jnp.where(even, z0, z1)
    own_lower = jnp.where(even, z1, z0)
    right_lower = jnp.where(even, got0, got1)
    left_upper = jnp.where(even, got1, got0)
    lane = iota((group, 128), 1)
    first = (lane & (LANES - 1)) < LANES // 2
    halo = jnp.where(first, right_lower + own_upper, left_upper + own_lower)
    inner = jnp.where(first, left_upper, right_lower)
    for g in range(GROUPS):
        count = min(group, planes * ROWS - g * group)
        low = pltpu.roll(inner, (-g * LANES) % 128, 1) if g else inner
        high = pltpu.roll(inner, (128 - LANES - g * LANES) % 128, 1)
        add = jnp.where(lane < LANES // 2, low, jnp.where(lane >= 128 - LANES // 2, high, 0.0))
        total = main_ref[g * group : g * group + count, :] + add[:count]
        out_ref[g * group : g * group + count, :] = total
        sent_ref[g * group : g * group + count, :] = total.astype(BF16)
    out_ref[planes * ROWS : planes * ROWS + group, :] = halo
    sent_ref[planes * ROWS : planes * ROWS + group, :] = halo.astype(BF16)


def y_fold_kernel(n_gy, units, tiles, group_planes, *refs):
    sources, (out_ref, far_ref) = refs[:n_gy], refs[n_gy:]
    half = iota((CY, 128), 0) < CY // 2
    wide = n_gy * CY
    planes = tiles + EXT
    for u in range(units):
        blocks = [None] * n_gy

        def add(b, value):
            b = b % n_gy
            blocks[b] = value if blocks[b] is None else blocks[b] + value

        for b, ref in enumerate(sources):
            both = ref[u * ROWS : (u + 1) * ROWS, :].astype(F32)
            add(b, both[:CY])
            rest = both[CY:]
            if n_gy == 2:
                add(b + 1, rest)
            else:
                add(b + 1, jnp.where(half, rest, 0.0))
                add(b - 1, jnp.where(half, 0.0, rest))
        value = jnp.concatenate(blocks, 0).astype(BF16)
        out_ref[u * wide : (u + 1) * wide, :] = value
        if u < EXT:
            far_ref[u * wide : (u + 1) * wide, :] = value
        elif planes - EXT <= u:
            v = u - (planes - EXT) + EXT
            far_ref[v * wide : (v + 1) * wide, :] = value


def field_kernel(
    tiles, chunks, group_planes, wide, span,
    own_ref, got1_ref, got3_ref, lower_ref, upper_ref, band_ref,
    charge_ref, offset_ref, cell_ref, potential_ref, force_ref, window, samples,
):
    planes = tiles + EXT
    radius = span // 2
    even = lax.rem(lax.axis_index("gx"), 2) == 0
    got1, got3 = got1_ref[...], got3_ref[...]
    right = jnp.where(even, got1, got3)
    left = jnp.where(even, got3, got1)
    own = own_ref[...]
    lane = iota((wide, 128), 1)
    margin = planes * wide

    def main(block, p):
        return block[p * wide : (p + 1) * wide].astype(F32)

    def edge(block, p, base=margin):
        g, q = divmod(p, group_planes)
        packed = block[base + q * wide : base + (q + 1) * wide].astype(F32)
        low = pltpu.roll(packed, (-g * LANES) % 128, 1) if g else packed
        high = pltpu.roll(packed, (128 - LANES - g * LANES) % 128, 1)
        return jnp.where(lane < LANES // 2, low, jnp.where(lane >= 128 - LANES // 2, high, 0.0))

    far_low, far_high = lower_ref[...], upper_ref[...]
    far_base = 2 * EXT * wide
    for x in range(2 * radius + planes):
        terms = []
        if x < planes:
            terms.append((main(left, x), edge(left, x)))
        if 0 <= x - tiles < planes:
            terms.append((main(own, x - tiles), edge(own, x - tiles)))
        if 0 <= x - 2 * tiles < planes:
            terms.append((main(right, x - 2 * tiles), edge(right, x - 2 * tiles)))
        if x < EXT:
            terms.append((main(far_low, EXT + x), edge(far_low, planes - EXT + x, far_base)))
        if 0 <= x - 3 * tiles < EXT:
            terms.append((main(far_high, x - 3 * tiles), edge(far_high, x - 3 * tiles, far_base)))
        window[x * wide : (x + 1) * wide, :128] = sum(a for a, _ in terms).astype(BF16)
        window[x * wide : (x + 1) * wide, 128:] = sum(b for _, b in terms).astype(BF16)

    band = band_ref[:, : span * wide]
    for x in range(planes):
        part = jnp.dot(
            band, window[x * wide : (x + span) * wide, :], preferred_element_type=F32
        )
        total = part[radius * ROWS : (radius + 1) * ROWS]
        for k in range(span):
            if k != radius:
                total = total + pltpu.roll(part[k * ROWS : (k + 1) * ROWS], (radius - k) % 256, 1)
        if 1 <= x <= tiles:
            potential_ref[x - 1] = total[:CY, :CZ]
        for c in range(4):
            moved = total if c == 1 else pltpu.roll(total, (1 - c) % 256, 1)
            samples[c, x * ROWS : (x + 1) * ROWS, :] = moved[:, :128]

    rows_total = tiles * chunks
    per = 8 // chunks
    upper_half = [iota((8, 128), 0) >= chunks * h for h in range(per)]
    for pair in range(tiles // per):
        rows = pl.ds(pair * 8, 8)
        charge = charge_ref[rows, :]
        xv, xs = spline(offset_ref[pl.ds(pair * 8, 8), :])
        yv, ys = spline(offset_ref[pl.ds(rows_total + pair * 8, 8), :])
        zv, zs = spline(offset_ref[pl.ds(2 * rows_total + pair * 8, 8), :])
        cy = cell_ref[pl.ds(pair * 8, 8), :] & (CY - 1)
        cz = cell_ref[pl.ds(rows_total + pair * 8, 8), :] & (CZ - 1)
        plain = [jnp.zeros((8, 128), F32) for _ in range(4)]
        along_y = [jnp.zeros((8, 128), F32) for _ in range(4)]
        along_z = [jnp.zeros((8, 128), F32) for _ in range(4)]
        for y in range(-1, CY + 2):
            distance = y + 1 - cy
            y_value = pick(distance, yv)
            y_slope = pick(distance, ys)
            row = y % ROWS
            for k in range(4):
                value = jnp.zeros((8, 128), F32)
                slope = jnp.zeros((8, 128), F32)
                for c in range(4):
                    source = None
                    for h in range(per):
                        at = (pair * per + h + k) * ROWS + row
                        line = jnp.broadcast_to(samples[c, at : at + 1, :], (8, 128))
                        source = line if h == 0 else jnp.where(upper_half[h], line, source)
                    picked = jnp.take_along_axis(source, cz, axis=1)
                    value = value + zv[c] * picked
                    slope = slope + zs[c] * picked
                plain[k] = plain[k] + y_value * value
                along_y[k] = along_y[k] + y_slope * value
                along_z[k] = along_z[k] + y_value * slope
        force_ref[0, rows, :] = -charge * sum(xs[k] * plain[k] for k in range(4))
        force_ref[1, rows, :] = -charge * sum(xv[k] * along_y[k] for k in range(4))
        force_ref[2, rows, :] = -charge * sum(xv[k] * along_z[k] for k in range(4))


def band_kernel(wide, kernel_ref, out_ref, rows_ref):
    span = kernel_ref.shape[0]
    radius = span // 2
    columns = out_ref.shape[1]
    base = jnp.zeros((span, columns), F32)
    tap = iota((span, columns), 0)
    column = iota((span, columns), 1)
    for i in range(span):
        place = jnp.where(
            (column >= i * wide) & (column < (i + 1) * wide)
            & (((column - tap + radius) & (wide - 1)) == 0),
            1.0, 0.0,
        ).astype(BF16)
        base = base + lax.dot_general(
            kernel_ref[i], place, (((0,), (0,)), ((), ())), preferred_element_type=F32
        )
    rows_ref[...] = jnp.zeros_like(rows_ref)
    within = column & (wide - 1)
    for y in range(-1, CY + 2):
        shift = y % wide
        moved = base
        if shift:
            moved = jnp.where(
                within >= shift,
                pltpu.roll(base, shift, 1),
                pltpu.roll(base, (shift - wide) % columns, 1),
            )
        for tile in range(columns // 128):
            rows_ref[tile, pl.ds(y % ROWS, span, stride=ROWS), :] = moved[:, tile * 128 : (tile + 1) * 128]
    for tile in range(columns // 128):
        out_ref[:, tile * 128 : (tile + 1) * 128] = rows_ref[tile].astype(BF16)


def vmem(n):
    return [pl.BlockSpec(memory_space=pltpu.VMEM)] * n


def local(charges, offsets, cells, kernel):
    n_gx, n_gy, n_gz = (lax.axis_size(axis) for axis in ("gx", "gy", "gz"))
    tiles, slots = charges.shape[0], charges.shape[3]
    span = kernel.shape[0]
    chunks = slots // 128
    rows = tiles * chunks
    planes = tiles + EXT
    group_planes = -(-planes // GROUPS)
    group = group_planes * ROWS
    wide = n_gy * CY
    band_columns = -(-span * wide // 128) * 128
    charge = charges.reshape(rows, 128)
    offset = offsets.reshape(3 * rows, 128)
    cell = cells.reshape(2 * rows, 128)

    def shape(*dims, kind=F32):
        return jax.ShapeDtypeStruct(dims, kind)

    near = lambda n: [(i, i ^ 1) for i in range(n)]
    other = lambda n: [(i, (i + 1 if i % 2 else i - 1) % n) for i in range(n)]
    shift = lambda n, s: [(i, (i + s) % n) for i in range(n)]

    z0, z1, s_high, s_low, weights, z_cell = pl.pallas_call(
        functools.partial(edge_kernel, tiles, chunks, group_planes),
        out_shape=(
            shape(group, 128), shape(group, 128),
            shape(tiles * 4 * ROWS, slots, kind=BF16), shape(tiles * 4 * ROWS, slots, kind=BF16),
            shape(8, rows, 128), shape(rows, 128, kind=jnp.int32),
        ),
        in_specs=[pl.BlockSpec(memory_space=pltpu.HBM)] * 3,
        out_specs=tuple(vmem(6)),
        scratch_shapes=[
            pltpu.VMEM((rows, 128), F32),
            pltpu.VMEM((3 * rows, 128), F32),
            pltpu.VMEM((2 * rows, 128), jnp.int32),
            pltpu.VMEM((4, rows, 128), F32),
            pltpu.VMEM((4, rows, 128), F32),
            pltpu.VMEM((GROUPS * group, 128), F32),
            pltpu.SemaphoreType.DMA((3,)),
        ],
        compiler_params=pltpu.CompilerParams(vmem_limit_bytes=8 << 20),
        name="edge",
    )(*(pltpu.with_memory_space_constraint(x, pltpu.HBM) for x in (charge, offset, cell)))
    got0 = lax.ppermute(z0, "gz", near(n_gz))
    got1 = lax.ppermute(z1, "gz", other(n_gz))
    main = pl.pallas_call(
        functools.partial(spread_kernel, tiles, chunks),
        out_shape=shape(planes * ROWS, 128),
        in_specs=vmem(4),
        out_specs=vmem(1)[0],
        compiler_params=pltpu.CompilerParams(vmem_limit_bytes=8 << 20),
        cost_estimate=pl.CostEstimate(flops=400_000_000, bytes_accessed=2_000_000, transcendentals=0),
        name="spread",
    )(s_high, s_low, weights, z_cell)
    units = planes + group_planes
    block, sent = pl.pallas_call(
        functools.partial(z_fold_kernel, tiles, group_planes),
        out_shape=(shape(units * ROWS, 128), shape(units * ROWS, 128, kind=BF16)),
        in_specs=vmem(5),
        out_specs=tuple(vmem(2)),
        compiler_params=pltpu.CompilerParams(vmem_limit_bytes=4 << 20),
        name="z_fold",
    )(main, z0, z1, got0, got1)
    sources = [block] + [lax.ppermute(sent, "gy", shift(n_gy, -s)) for s in range(1, n_gy)]
    mine, far = pl.pallas_call(
        functools.partial(y_fold_kernel, n_gy, units, tiles, group_planes),
        out_shape=(shape(units * wide, 128, kind=BF16), shape((2 * EXT + group_planes) * wide, 128, kind=BF16)),
        in_specs=vmem(n_gy),
        out_specs=tuple(vmem(2)),
        compiler_params=pltpu.CompilerParams(vmem_limit_bytes=4 << 20),
        name="y_fold",
    )(*sources)
    x1 = lax.ppermute(mine, "gx", near(n_gx))
    if n_gx == 4:
        lower = upper = lax.ppermute(far, "gx", shift(n_gx, 2))
    else:
        lower = lax.ppermute(far, "gx", shift(n_gx, 2))
        upper = lax.ppermute(far, "gx", shift(n_gx, -2))
    x3 = lax.ppermute(mine, "gx", other(n_gx))
    band = pl.pallas_call(
        functools.partial(band_kernel, wide),
        out_shape=shape(span * ROWS, band_columns, kind=BF16),
        in_specs=vmem(1),
        out_specs=vmem(1)[0],
        scratch_shapes=[pltpu.VMEM((band_columns // 128, span * ROWS, 128), F32)],
        compiler_params=pltpu.CompilerParams(vmem_limit_bytes=8 << 20),
        name="band",
    )(kernel)
    potential, forces = pl.pallas_call(
        functools.partial(field_kernel, tiles, chunks, group_planes, wide, span),
        out_shape=(shape(tiles, CY, CZ), shape(3, rows, 128)),
        in_specs=vmem(9),
        out_specs=tuple(vmem(2)),
        scratch_shapes=[
            pltpu.VMEM(((2 * (span // 2) + planes) * wide, 256), BF16),
            pltpu.VMEM((4, planes * ROWS, 128), F32),
        ],
        compiler_params=pltpu.CompilerParams(vmem_limit_bytes=16 << 20),
        name="field",
    )(mine, x1, x3, lower, upper, band, charge, offset, cell)
    return potential, forces.reshape(3, tiles, 1, 1, slots)


def solution(mesh):
    placed = (
        P("gx", "gy", "gz", None),
        P(None, "gx", "gy", "gz", None),
        P(None, "gx", "gy", "gz", None),
        P(),
    )
    return jax.shard_map(
        local,
        mesh=mesh,
        in_specs=placed,
        out_specs=(P("gx", "gy", "gz"), P(None, "gx", "gy", "gz", None)),
        check_vma=False,
    )
```

```python
import functools

import jax
import jax.numpy as jnp
from jax import lax
from jax.experimental import pallas as pl
from jax.experimental.pallas import tpu as pltpu
from jax.sharding import PartitionSpec as P


CY = 8
CZ = 128
EXT = 3
ROWS = 16
TALL = CY + EXT
AHEAD = 4
LANES = 32
GROUPS = 128 // LANES

F32 = jnp.float32
BF16 = jnp.bfloat16


def spline(fraction):
    remain = 1.0 - fraction
    values = [
        remain**3 / 6.0,
        (3.0 * fraction**3 - 6.0 * fraction**2 + 4.0) / 6.0,
        (-3.0 * fraction**3 + 3.0 * fraction**2 + 3.0 * fraction + 1.0) / 6.0,
        fraction**3 / 6.0,
    ]
    slopes = [
        -0.5 * remain**2,
        1.5 * fraction**2 - 2.0 * fraction,
        -1.5 * fraction**2 + fraction + 0.5,
        0.5 * fraction**2,
    ]
    return values, slopes


def pick(distance, four):
    out = jnp.zeros((), F32)
    for c in reversed(range(4)):
        out = jnp.where(distance == c, four[c], out)
    return out


def split(x):
    high = x.astype(BF16)
    return high, (x - high.astype(F32)).astype(BF16)


def nt_dot(a, b):
    return lax.dot_general(a, b, (((1,), (1,)), ((), ())), preferred_element_type=F32)


def iota(shape, dim, kind=jnp.int32):
    return lax.broadcasted_iota(kind, shape, dim)


def tall(row, kind, count):
    tile = jnp.broadcast_to(row, (16, 128)).astype(kind)
    return jnp.concatenate([tile] * (count // 16), 0)


def z_weights(z_of_row, cell, rows):
    count = z_of_row.shape[0]
    high = low = jnp.zeros((count, 128), BF16)
    for c in range(4):
        here = z_of_row == tall(cell + (c - 1), jnp.int16, count)
        high = jnp.where(here, tall(rows[c], BF16, count), high)
        low = jnp.where(here, tall(rows[4 + c], BF16, count), low)
    return high, low


def edge_kernel(
    tiles, chunks, group_planes, charge_hbm, offset_hbm, cell_hbm,
    z0_ref, z1_ref, high_ref, low_ref, weight_ref, cell_ref,
    charge_in, offset_in, cell_in, x_rows, y_rows, acc, sems,
):
    copies = [
        pltpu.make_async_copy(source, target, sems.at[n])
        for n, (source, target) in enumerate(
            ((charge_hbm, charge_in), (offset_hbm, offset_in), (cell_hbm, cell_in))
        )
    ]
    for copy in copies:
        copy.start()
    rows = tiles * chunks
    acc[...] = jnp.zeros_like(acc)
    row = iota((2 * LANES, 128), 0, jnp.int16)
    z_of_row = row - LANES // 2 + jnp.where(row < LANES, jnp.int16(0), jnp.int16(CZ - LANES))
    y_row = iota((ROWS, 128), 0)
    y_of_row = jnp.where(y_row < 12, y_row, y_row - ROWS)
    for copy in copies:
        copy.wait()
    for r in range(0, rows, 8):
        at = pl.ds(r, 8)
        xv, _ = spline(offset_in[at, :])
        yv, _ = spline(offset_in[pl.ds(rows + r, 8), :])
        zv, _ = spline(offset_in[pl.ds(2 * rows + r, 8), :])
        charge = charge_in[at, :]
        for c in range(4):
            x_rows[c, at, :] = charge * xv[c]
            y_rows[c, at, :] = yv[c]
            high = zv[c].astype(BF16).astype(F32)
            weight_ref[c, at, :] = high
            weight_ref[4 + c, at, :] = zv[c] - high
        cell_ref[at, :] = cell_in[pl.ds(rows + r, 8), :] & (CZ - 1)
    for t in range(tiles):
        parts = [], [], [], []
        for j in range(chunks):
            at = pl.ds(t * chunks + j, 1)
            cy = cell_in[at, :] & (CY - 1)
            y_dense = pick(y_of_row - (cy - 1), [y_rows[c, at, :] for c in range(4)])
            s = jnp.concatenate([y_dense * x_rows[k, at, :] for k in range(4)], 0)
            z = z_weights(z_of_row, cell_ref[at, :], [weight_ref[c, at, :] for c in range(8)])
            for part, value in zip(parts, split(s) + z):
                part.append(value)
        s_high, s_low, z_high, z_low = (jnp.concatenate(part, 1) for part in parts)
        high_ref[t * 4 * ROWS : (t + 1) * 4 * ROWS, :] = s_high
        low_ref[t * 4 * ROWS : (t + 1) * 4 * ROWS, :] = s_low
        both = nt_dot(jnp.concatenate([s_high, s_low], 0), z_high)
        got = both[: 4 * ROWS] + both[4 * ROWS :] + nt_dot(s_high, z_low)
        acc[t * ROWS : (t + 4) * ROWS, : 2 * LANES] += got
    group = group_planes * ROWS
    lane = iota((group, 128), 1)
    lower_out = jnp.zeros((group, 128), F32)
    upper_out = jnp.zeros((group, 128), F32)
    for g in range(GROUPS):
        edge = acc[g * group : (g + 1) * group, :]
        low = jnp.where(lane < LANES, edge, 0.0)
        high = jnp.where(lane >= LANES, edge, 0.0)
        lower_out = lower_out + pltpu.roll(low, (g * LANES - LANES // 2) % 128, 1)
        upper_out = upper_out + pltpu.roll(high, (g * LANES - LANES // 2 - LANES) % 128, 1)
    even = lax.rem(lax.axis_index("gz"), 2) == 0
    z0_ref[...] = jnp.where(even, upper_out, lower_out)
    z1_ref[...] = jnp.where(even, lower_out, upper_out)


def spread_kernel(tiles, chunks, high_ref, low_ref, weight_ref, cell_ref, main_ref):
    main_ref[...] = jnp.zeros_like(main_ref)
    z_of_row = iota((CZ, 128), 0, jnp.int16)
    for t in range(tiles):
        parts = [], []
        for j in range(chunks):
            at = pl.ds(t * chunks + j, 1)
            z = z_weights(z_of_row, cell_ref[at, :], [weight_ref[c, at, :] for c in range(8)])
            for part, value in zip(parts, z):
                part.append(value)
        z_high, z_low = (jnp.concatenate(part, 1) for part in parts)
        s_high = high_ref[t * 4 * ROWS : (t + 1) * 4 * ROWS, :]
        s_low = low_ref[t * 4 * ROWS : (t + 1) * 4 * ROWS, :]
        both = nt_dot(jnp.concatenate([s_high, s_low], 0), z_high)
        got = both[: 4 * ROWS] + both[4 * ROWS :] + nt_dot(s_high, z_low)
        main_ref[t * ROWS : (t + 4) * ROWS, :] += got


def z_fold_kernel(tiles, group_planes, main_ref, z0_ref, z1_ref, got0_ref, got1_ref, out_ref, sent_ref):
    planes = tiles + EXT
    group = group_planes * ROWS
    units = []
    even = lax.rem(lax.axis_index("gz"), 2) == 0
    z0, z1, got0, got1 = z0_ref[...], z1_ref[...], got0_ref[...], got1_ref[...]
    own_upper = jnp.where(even, z0, z1)
    own_lower = jnp.where(even, z1, z0)
    right_lower = jnp.where(even, got0, got1)
    left_upper = jnp.where(even, got1, got0)
    lane = iota((group, 128), 1)
    first = ((lane + LANES // 2) & (LANES - 1)) >= LANES // 2
    rim = (lane < LANES // 2) | (lane >= 128 - LANES // 2)
    halo = jnp.where(first, right_lower + own_upper, left_upper + own_lower)
    inner = jnp.where(first, left_upper, right_lower)
    for g in range(GROUPS):
        count = min(group, planes * ROWS - g * group)
        add = jnp.where(rim, pltpu.roll(inner, (-g * LANES) % 128, 1) if g else inner, 0.0)
        total = main_ref[g * group : g * group + count, :] + add[:count]
        out_ref[g * group : g * group + count, :] = total
        units += [total[at : at + ROWS] for at in range(0, count, ROWS)]
    out_ref[planes * ROWS : planes * ROWS + group, :] = halo
    units += [halo[at : at + ROWS] for at in range(0, group, ROWS)]
    inner = [unit[:CY] for unit in units]
    outer = [unit[CY:] for unit in units]
    outer = [
        pair[0] + pltpu.roll(pair[1], CY // 2, 0) if len(pair) > 1 else pair[0]
        for pair in (outer[u : u + 2] for u in range(0, len(outer), 2))
    ]
    halves = inner + outer
    halves += [jnp.zeros((CY, 128), F32)] * (len(halves) % 2)
    for u in range(0, len(halves), 2):
        sent_ref[u * CY : (u + 2) * CY, :] = jnp.concatenate(halves[u : u + 2], 0).astype(BF16)


def y_fold_kernel(n_gy, units, tiles, *refs):
    sources, (out_ref, far_ref) = refs[:n_gy], refs[n_gy:]
    half = iota((CY, 128), 0) < CY // 2
    filled = (iota((CY, 128), 0) < 2) | (iota((CY, 128), 0) == CY - 1)
    values = [ref[...].astype(F32) for ref in sources]
    wide = n_gy * CY
    planes = tiles + EXT
    for u in range(units):
        blocks = [None] * n_gy

        def add(b, value):
            b = b % n_gy
            blocks[b] = value if blocks[b] is None else blocks[b] + value

        for b, value in enumerate(values):
            if b == 0:
                first = value[u * ROWS : u * ROWS + CY]
                rest = value[u * ROWS + CY : (u + 1) * ROWS]
            else:
                first = value[u * CY : (u + 1) * CY]
                at = (units + u // 2) * CY
                rest = value[at : at + CY]
                rest = jnp.where(filled, pltpu.roll(rest, CY // 2, 0) if u % 2 else rest, 0.0)
            add(b, first)
            if n_gy == 2:
                add(b + 1, rest)
            else:
                add(b + 1, jnp.where(half, rest, 0.0))
                add(b - 1, jnp.where(half, 0.0, rest))
        value = jnp.concatenate(blocks, 0).astype(BF16)
        out_ref[u * wide : (u + 1) * wide, :] = value
        if u < EXT:
            far_ref[u * wide : (u + 1) * wide, :] = value
        elif planes - EXT <= u:
            v = u - (planes - EXT) + EXT
            far_ref[v * wide : (v + 1) * wide, :] = value


def field_kernel(
    tiles, chunks, group_planes, wide, span,
    own_ref, got1_ref, got3_ref, lower_ref, upper_ref, band_ref, y_ref,
    charge_ref, offset_ref, cell_ref, potential_ref, force_ref, window, parts, samples,
):
    planes = tiles + EXT
    radius = span // 2
    even = lax.rem(lax.axis_index("gx"), 2) == 0
    got1, got3 = got1_ref[...], got3_ref[...]
    right = jnp.where(even, got1, got3)
    left = jnp.where(even, got3, got1)
    own = own_ref[...]
    margin = planes * wide
    lane = iota((wide, 128), 1)
    rim = (lane < LANES // 2) | (lane >= 128 - LANES // 2)

    def main(block, p):
        return block[p * wide : (p + 1) * wide].astype(F32)

    def edge(block, p, base=margin):
        g, q = divmod(p, group_planes)
        packed = block[base + q * wide : base + (q + 1) * wide].astype(F32)
        return pltpu.roll(packed, (-g * LANES) % 128, 1) if g else packed

    far_low, far_high = lower_ref[...], upper_ref[...]
    far_base = 2 * EXT * wide
    for x in range(2 * radius + planes):
        terms = []
        if x < planes:
            terms.append((main(left, x), edge(left, x)))
        if 0 <= x - tiles < planes:
            terms.append((main(own, x - tiles), edge(own, x - tiles)))
        if 0 <= x - 2 * tiles < planes:
            terms.append((main(right, x - 2 * tiles), edge(right, x - 2 * tiles)))
        if x < EXT:
            terms.append((main(far_low, EXT + x), edge(far_low, planes - EXT + x, far_base)))
        if 0 <= x - 3 * tiles < EXT:
            terms.append((main(far_high, x - 3 * tiles), edge(far_high, x - 3 * tiles, far_base)))
        window[x * wide : (x + 1) * wide, :128] = sum(a for a, _ in terms).astype(BF16)
        window[x * wide : (x + 1) * wide, 128:] = jnp.where(
            rim, sum(b for _, b in terms), 0.0
        ).astype(BF16)

    taps = span * ROWS
    for x in range(0, planes, AHEAD):
        count = min(AHEAD, planes - x)
        part = jnp.dot(
            band_ref[: count * taps, : (span + count - 1) * wide],
            window[x * wide : (x + span + count - 1) * wide, :],
            preferred_element_type=F32,
        )
        for n in range(count):
            for k in range(span):
                at = n * taps + k * ROWS
                parts[k, (x + n) * TALL : (x + n + 1) * TALL, :] = part[at : at + TALL]
    lane = iota((8, 128), 1)
    for row in range(0, planes * TALL, 8):
        total = parts[radius, row : row + 8, :128]
        outside = [None] * 3
        for k in range(span):
            inner = parts[k, row : row + 8, :128]
            outer = parts[k, row : row + 8, 128:]
            step = radius - k
            if step:
                taken = lane >= 128 - step if step > 0 else lane < -step
                total = total + pltpu.roll(jnp.where(taken, outer, inner), step % 128, 1)
            for n, z in enumerate((-1, CZ, CZ + 1)):
                at = z - step
                value = inner if 0 <= at < CZ else outer
                old = 0.0 if outside[n] is None else outside[n]
                outside[n] = jnp.where(lane == at % 128, value, old)
        below, above, beyond = (jnp.sum(v, axis=1, keepdims=True) for v in outside)
        samples[0, row : row + 8, :] = jnp.where(lane == 0, below, pltpu.roll(total, 1, 1))
        samples[1, row : row + 8, :] = total
        samples[2, row : row + 8, :] = jnp.where(lane == CZ - 1, above, pltpu.roll(total, 127, 1))
        samples[3, row : row + 8, :] = jnp.where(
            lane == CZ - 1, beyond, jnp.where(lane == CZ - 2, above, pltpu.roll(total, 126, 1))
        )
    for x in range(tiles):
        potential_ref[x] = samples[1, (x + 1) * TALL + 1 : (x + 1) * TALL + 1 + CY, :]

    rows_total = tiles * chunks
    per = 8 // chunks
    pairs = tiles // per
    upper_half = [iota((8, 128), 0) >= chunks * h for h in range(per)]
    for p in range(pairs):
        at = pl.ds(p * 8, 8)
        cz = cell_ref[pl.ds(rows_total + p * 8, 8), :] & (CZ - 1)
        zv, zs = spline(offset_ref[pl.ds(2 * rows_total + p * 8, 8), :])
        xv, xs = spline(offset_ref[at, :])
        force = [jnp.zeros((8, 128), F32)] * 3
        for k in range(4):
            plain = [jnp.zeros((8, 128), F32)] * 4
            sloped = [jnp.zeros((8, 128), F32)] * 4
            for y in range(TALL):
                y_at = pl.ds((p * TALL + y) * 8, 8)
                y_value = y_ref[0, y_at, :]
                y_slope = y_ref[1, y_at, :]
                for c in range(4):
                    source = None
                    for h in range(per):
                        row = (p * per + k + h) * TALL + y
                        line = jnp.broadcast_to(samples[c, row : row + 1, :], (8, 128))
                        source = line if h == 0 else jnp.where(upper_half[h], line, source)
                    picked = jnp.take_along_axis(source, cz, axis=1)
                    plain[c] = plain[c] + y_value * picked
                    sloped[c] = sloped[c] + y_slope * picked
            value = sum(zv[c] * plain[c] for c in range(4))
            along_y = sum(zv[c] * sloped[c] for c in range(4))
            along_z = sum(zs[c] * plain[c] for c in range(4))
            force[0] = force[0] + xs[k] * value
            force[1] = force[1] + xv[k] * along_y
            force[2] = force[2] + xv[k] * along_z
        charge = charge_ref[at, :]
        for d in range(3):
            force_ref[d, at, :] = -charge * force[d]


def band_kernel(tiles, chunks, wide, kernel_ref, offset_ref, cell_ref, out_ref, y_ref, rows_ref):
    rows_total = tiles * chunks
    for p in range(rows_total // 8):
        yv, ys = spline(offset_ref[pl.ds(rows_total + p * 8, 8), :])
        cy = cell_ref[pl.ds(p * 8, 8), :] & (CY - 1)
        for y in range(TALL):
            at = pl.ds((p * TALL + y) * 8, 8)
            y_ref[0, at, :] = pick(y - cy, yv)
            y_ref[1, at, :] = pick(y - cy, ys)
    span = kernel_ref.shape[0]
    radius = span // 2
    columns = out_ref.shape[1]
    base = jnp.zeros((span, columns), F32)
    tap = iota((span, columns), 0)
    column = iota((span, columns), 1)
    for i in range(span):
        place = jnp.where(
            (column >= i * wide) & (column < (i + 1) * wide)
            & (((column - tap + radius) & (wide - 1)) == 0),
            1.0, 0.0,
        ).astype(BF16)
        base = base + lax.dot_general(
            kernel_ref[i], place, (((0,), (0,)), ((), ())), preferred_element_type=F32
        )
    rows_ref[...] = jnp.zeros_like(rows_ref)
    within = column & (wide - 1)
    for y in range(-1, CY + 2):
        shift = y % wide
        moved = base
        if shift:
            moved = jnp.where(
                within >= shift,
                pltpu.roll(base, shift, 1),
                pltpu.roll(base, (shift - wide) % columns, 1),
            )
        for tile in range(columns // 128):
            rows_ref[tile, pl.ds(y + 1, span, stride=ROWS), :] = moved[:, tile * 128 : (tile + 1) * 128]
    taps = span * ROWS
    for n in range(AHEAD):
        for tile in range(columns // 128):
            value = rows_ref[tile]
            if n:
                before = rows_ref[tile - 1] if tile else jnp.zeros_like(value)
                shift = n * wide
                value = jnp.where(
                    iota(value.shape, 1) < shift,
                    pltpu.roll(before, shift, 1),
                    pltpu.roll(value, shift, 1),
                )
            out_ref[n * taps : (n + 1) * taps, tile * 128 : (tile + 1) * 128] = value.astype(BF16)


def vmem(n):
    return [pl.BlockSpec(memory_space=pltpu.VMEM)] * n


def local(charges, offsets, cells, kernel):
    n_gx, n_gy, n_gz = (lax.axis_size(axis) for axis in ("gx", "gy", "gz"))
    tiles, slots = charges.shape[0], charges.shape[3]
    span = kernel.shape[0]
    chunks = slots // 128
    rows = tiles * chunks
    planes = tiles + EXT
    group_planes = -(-planes // GROUPS)
    group = group_planes * ROWS
    wide = n_gy * CY
    band_columns = -(-(span + AHEAD - 1) * wide // 128) * 128
    charge = charges.reshape(rows, 128)
    offset = offsets.reshape(3 * rows, 128)
    cell = cells.reshape(2 * rows, 128)

    def shape(*dims, kind=F32):
        return jax.ShapeDtypeStruct(dims, kind)

    near = lambda n: [(i, i ^ 1) for i in range(n)]
    other = lambda n: [(i, (i + 1 if i % 2 else i - 1) % n) for i in range(n)]
    shift = lambda n, s: [(i, (i + s) % n) for i in range(n)]

    z0, z1, s_high, s_low, weights, z_cell = pl.pallas_call(
        functools.partial(edge_kernel, tiles, chunks, group_planes),
        out_shape=(
            shape(group, 128), shape(group, 128),
            shape(tiles * 4 * ROWS, slots, kind=BF16), shape(tiles * 4 * ROWS, slots, kind=BF16),
            shape(8, rows, 128), shape(rows, 128, kind=jnp.int32),
        ),
        in_specs=[pl.BlockSpec(memory_space=pltpu.HBM)] * 3,
        out_specs=tuple(vmem(6)),
        scratch_shapes=[
            pltpu.VMEM((rows, 128), F32),
            pltpu.VMEM((3 * rows, 128), F32),
            pltpu.VMEM((2 * rows, 128), jnp.int32),
            pltpu.VMEM((4, rows, 128), F32),
            pltpu.VMEM((4, rows, 128), F32),
            pltpu.VMEM((GROUPS * group, 128), F32),
            pltpu.SemaphoreType.DMA((3,)),
        ],
        compiler_params=pltpu.CompilerParams(vmem_limit_bytes=8 << 20),
        name="edge",
    )(*(pltpu.with_memory_space_constraint(x, pltpu.HBM) for x in (charge, offset, cell)))
    got0 = lax.ppermute(z0, "gz", near(n_gz))
    got1 = lax.ppermute(z1, "gz", other(n_gz))
    main = pl.pallas_call(
        functools.partial(spread_kernel, tiles, chunks),
        out_shape=shape(planes * ROWS, 128),
        in_specs=vmem(4),
        out_specs=vmem(1)[0],
        compiler_params=pltpu.CompilerParams(vmem_limit_bytes=8 << 20),
        cost_estimate=pl.CostEstimate(flops=400_000_000, bytes_accessed=2_000_000, transcendentals=0),
        name="spread",
    )(s_high, s_low, weights, z_cell)
    units = planes + group_planes
    block, sent = pl.pallas_call(
        functools.partial(z_fold_kernel, tiles, group_planes),
        out_shape=(shape(units * ROWS, 128), shape(-(-(units + -(-units // 2)) // 2) * 2 * CY, 128, kind=BF16)),
        in_specs=vmem(5),
        out_specs=tuple(vmem(2)),
        compiler_params=pltpu.CompilerParams(vmem_limit_bytes=4 << 20),
        name="z_fold",
    )(main, z0, z1, got0, got1)
    sources = [block] + [lax.ppermute(sent, "gy", shift(n_gy, -s)) for s in range(1, n_gy)]
    mine, far = pl.pallas_call(
        functools.partial(y_fold_kernel, n_gy, units, tiles),
        out_shape=(shape(units * wide, 128, kind=BF16), shape((2 * EXT + group_planes) * wide, 128, kind=BF16)),
        in_specs=vmem(n_gy),
        out_specs=tuple(vmem(2)),
        compiler_params=pltpu.CompilerParams(vmem_limit_bytes=4 << 20),
        name="y_fold",
    )(*sources)
    x1 = lax.ppermute(mine, "gx", near(n_gx))
    lower = lax.ppermute(far, "gx", shift(n_gx, 2))
    upper = lower
    if n_gx != 4:
        upper = lax.ppermute(far, "gx", shift(n_gx, -2))
    x3 = lax.ppermute(mine, "gx", other(n_gx))
    band, y_dense = pl.pallas_call(
        functools.partial(band_kernel, tiles, chunks, wide),
        out_shape=(
            shape(AHEAD * span * ROWS, band_columns, kind=BF16),
            shape(2, rows * TALL, 128),
        ),
        in_specs=vmem(3),
        out_specs=tuple(vmem(2)),
        scratch_shapes=[pltpu.VMEM((band_columns // 128, span * ROWS, 128), F32)],
        compiler_params=pltpu.CompilerParams(vmem_limit_bytes=8 << 20),
        cost_estimate=pl.CostEstimate(flops=400_000_000, bytes_accessed=2_000_000, transcendentals=0),
        name="band",
    )(kernel, offset, cell)
    potential, forces = pl.pallas_call(
        functools.partial(field_kernel, tiles, chunks, group_planes, wide, span),
        out_shape=(shape(tiles, CY, CZ), shape(3, rows, 128)),
        in_specs=vmem(10),
        out_specs=tuple(vmem(2)),
        scratch_shapes=[
            pltpu.VMEM(((2 * (span // 2) + planes) * wide, 256), BF16),
            pltpu.VMEM((span, -(-planes * TALL // 8) * 8, 256), F32),
            pltpu.VMEM((4, -(-planes * TALL // 8) * 8, 128), F32),
        ],
        compiler_params=pltpu.CompilerParams(vmem_limit_bytes=16 << 20),
        name="field",
    )(mine, x1, x3, lower, upper, band, y_dense, charge, offset, cell)
    return potential, forces.reshape(3, tiles, 1, 1, slots)


def solution(mesh):
    placed = (
        P("gx", "gy", "gz", None),
        P(None, "gx", "gy", "gz", None),
        P(None, "gx", "gy", "gz", None),
        P(),
    )
    return jax.shard_map(
        local,
        mesh=mesh,
        in_specs=placed,
        out_specs=(P("gx", "gy", "gz"), P(None, "gx", "gy", "gz", None)),
        check_vma=False,
    )
```

```python
import functools

import jax
import jax.numpy as jnp
from jax import lax
from jax.experimental import pallas as pl
from jax.experimental.pallas import tpu as pltpu
from jax.sharding import PartitionSpec as P


CY = 8
CZ = 128
EXT = 3
ROWS = 16
TALL = CY + EXT
AHEAD = 4
STEP = -(-AHEAD * TALL // 8) * 8
LANES = 32
GROUPS = 128 // LANES

F32 = jnp.float32
BF16 = jnp.bfloat16


def spline(fraction):
    remain = 1.0 - fraction
    values = [
        remain**3 / 6.0,
        (3.0 * fraction**3 - 6.0 * fraction**2 + 4.0) / 6.0,
        (-3.0 * fraction**3 + 3.0 * fraction**2 + 3.0 * fraction + 1.0) / 6.0,
        fraction**3 / 6.0,
    ]
    slopes = [
        -0.5 * remain**2,
        1.5 * fraction**2 - 2.0 * fraction,
        -1.5 * fraction**2 + fraction + 0.5,
        0.5 * fraction**2,
    ]
    return values, slopes


def pick(distance, four):
    out = jnp.zeros((), F32)
    for c in reversed(range(4)):
        out = jnp.where(distance == c, four[c], out)
    return out


def split(x):
    high = x.astype(BF16)
    return high, (x - high.astype(F32)).astype(BF16)


def nt_dot(a, b):
    return lax.dot_general(a, b, (((1,), (1,)), ((), ())), preferred_element_type=F32)


def iota(shape, dim, kind=jnp.int32):
    return lax.broadcasted_iota(kind, shape, dim)


def tall(row, kind, count):
    tile = jnp.broadcast_to(row, (16, 128)).astype(kind)
    return jnp.concatenate([tile] * (count // 16), 0)


def z_weights(z_of_row, cell, rows):
    count = z_of_row.shape[0]
    high = low = jnp.zeros((count, 128), BF16)
    for c in range(4):
        here = z_of_row == tall(cell + (c - 1), jnp.int16, count)
        high = jnp.where(here, tall(rows[c], BF16, count), high)
        low = jnp.where(here, tall(rows[4 + c], BF16, count), low)
    return high, low


def edge_kernel(
    tiles, chunks, group_planes, charge_hbm, offset_hbm, cell_hbm,
    z0_ref, z1_ref, high_ref, low_ref, weight_ref, cell_ref,
    charge_in, offset_in, cell_in, x_rows, y_rows, acc, sems,
):
    copies = [
        pltpu.make_async_copy(source, target, sems.at[n])
        for n, (source, target) in enumerate(
            ((charge_hbm, charge_in), (offset_hbm, offset_in), (cell_hbm, cell_in))
        )
    ]
    for copy in copies:
        copy.start()
    rows = tiles * chunks
    acc[...] = jnp.zeros_like(acc)
    row = iota((LANES, 128), 0, jnp.int16)
    z_of_row = jnp.where(row < LANES // 2, row - 1, row + (CZ + 2 - LANES // 2 - 11))
    y_row = iota((ROWS, 128), 0)
    y_of_row = jnp.where(y_row < 12, y_row, y_row - ROWS)
    for copy in copies:
        copy.wait()
    for r in range(0, rows, 8):
        at = pl.ds(r, 8)
        xv, _ = spline(offset_in[at, :])
        yv, _ = spline(offset_in[pl.ds(rows + r, 8), :])
        zv, _ = spline(offset_in[pl.ds(2 * rows + r, 8), :])
        charge = charge_in[at, :]
        for c in range(4):
            x_rows[c, at, :] = charge * xv[c]
            y_rows[c, at, :] = yv[c]
            high = zv[c].astype(BF16).astype(F32)
            weight_ref[c, at, :] = high
            weight_ref[4 + c, at, :] = zv[c] - high
        cell_ref[at, :] = cell_in[pl.ds(rows + r, 8), :] & (CZ - 1)
    for t in range(tiles):
        parts = [], [], [], []
        for j in range(chunks):
            at = pl.ds(t * chunks + j, 1)
            cy = cell_in[at, :] & (CY - 1)
            y_dense = pick(y_of_row - (cy - 1), [y_rows[c, at, :] for c in range(4)])
            s = jnp.concatenate([y_dense * x_rows[k, at, :] for k in range(4)], 0)
            z = z_weights(z_of_row, cell_ref[at, :], [weight_ref[c, at, :] for c in range(8)])
            for part, value in zip(parts, split(s) + z):
                part.append(value)
        s_high, s_low, z_high, z_low = (jnp.concatenate(part, 1) for part in parts)
        high_ref[t * 4 * ROWS : (t + 1) * 4 * ROWS, :] = s_high
        low_ref[t * 4 * ROWS : (t + 1) * 4 * ROWS, :] = s_low
        both = nt_dot(jnp.concatenate([s_high, s_low], 0), z_high)
        got = both[: 4 * ROWS] + both[4 * ROWS :] + nt_dot(s_high, z_low)
        acc[t * ROWS : (t + 4) * ROWS, :LANES] += got
    group = group_planes * ROWS
    lane = iota((group, 128), 1)
    lower_out = jnp.zeros((group, 128), F32)
    upper_out = jnp.zeros((group, 128), F32)
    for g in range(GROUPS):
        edge = acc[g * group : (g + 1) * group, :]
        low = jnp.where(lane < LANES // 2, edge, 0.0)
        high = jnp.where(lane >= LANES // 2, edge, 0.0)
        lower_out = lower_out + pltpu.roll(low, (g * LANES - 1) % 128, 1)
        upper_out = upper_out + pltpu.roll(high, (g * LANES - LANES // 2 - 9) % 128, 1)
    even = lax.rem(lax.axis_index("gz"), 2) == 0
    z0_ref[...] = jnp.where(even, upper_out, lower_out).astype(BF16)
    z1_ref[...] = jnp.where(even, lower_out, upper_out).astype(BF16)


def spread_kernel(tiles, chunks, high_ref, low_ref, weight_ref, cell_ref, main_ref):
    main_ref[...] = jnp.zeros_like(main_ref)
    z_of_row = iota((CZ, 128), 0, jnp.int16)
    for t in range(tiles):
        parts = [], []
        for j in range(chunks):
            at = pl.ds(t * chunks + j, 1)
            z = z_weights(z_of_row, cell_ref[at, :], [weight_ref[c, at, :] for c in range(8)])
            for part, value in zip(parts, z):
                part.append(value)
        z_high, z_low = (jnp.concatenate(part, 1) for part in parts)
        s_high = high_ref[t * 4 * ROWS : (t + 1) * 4 * ROWS, :]
        s_low = low_ref[t * 4 * ROWS : (t + 1) * 4 * ROWS, :]
        both = nt_dot(jnp.concatenate([s_high, s_low], 0), z_high)
        got = both[: 4 * ROWS] + both[4 * ROWS :] + nt_dot(s_high, z_low)
        main_ref[t * ROWS : (t + 4) * ROWS, :] += got


def z_fold_kernel(tiles, group_planes, main_ref, z0_ref, z1_ref, got0_ref, got1_ref, out_ref, sent_ref):
    planes = tiles + EXT
    group = group_planes * ROWS
    units = []
    even = lax.rem(lax.axis_index("gz"), 2) == 0
    z0, z1, got0, got1 = (ref[...].astype(F32) for ref in (z0_ref, z1_ref, got0_ref, got1_ref))
    own_upper = jnp.where(even, z0, z1)
    own_lower = jnp.where(even, z1, z0)
    right_lower = jnp.where(even, got0, got1)
    left_upper = jnp.where(even, got1, got0)
    lane = iota((group, 128), 1)
    first = ((lane + LANES // 2) & (LANES - 1)) >= LANES // 2
    rim = (lane < LANES // 2) | (lane >= 128 - LANES // 2)
    halo = jnp.where(first, right_lower + own_upper, left_upper + own_lower)
    inner = jnp.where(first, left_upper, right_lower)
    for g in range(GROUPS):
        count = min(group, planes * ROWS - g * group)
        add = jnp.where(rim, pltpu.roll(inner, (-g * LANES) % 128, 1) if g else inner, 0.0)
        total = main_ref[g * group : g * group + count, :] + add[:count]
        out_ref[g * group : g * group + count, :] = total
        units += [total[at : at + ROWS] for at in range(0, count, ROWS)]
    out_ref[planes * ROWS : planes * ROWS + group, :] = halo
    units += [halo[at : at + ROWS] for at in range(0, group, ROWS)]
    inner = [unit[:CY] for unit in units]
    outer = [unit[CY:] for unit in units]
    outer = [
        pair[0] + pltpu.roll(pair[1], CY // 2, 0) if len(pair) > 1 else pair[0]
        for pair in (outer[u : u + 2] for u in range(0, len(outer), 2))
    ]
    halves = inner + outer
    halves += [jnp.zeros((CY, 128), F32)] * (len(halves) % 2)
    for u in range(0, len(halves), 2):
        sent_ref[u * CY : (u + 2) * CY, :] = jnp.concatenate(halves[u : u + 2], 0).astype(BF16)


def y_fold_kernel(n_gy, units, tiles, *refs):
    sources, (out_ref, far_ref, exact_ref) = refs[:n_gy], refs[n_gy:]
    half = iota((CY, 128), 0) < CY // 2
    filled = (iota((CY, 128), 0) < 2) | (iota((CY, 128), 0) == CY - 1)
    values = [ref[...].astype(F32) for ref in sources]
    wide = n_gy * CY
    planes = tiles + EXT
    for u in range(units):
        blocks = [None] * n_gy

        def add(b, value):
            b = b % n_gy
            blocks[b] = value if blocks[b] is None else blocks[b] + value

        for b, value in enumerate(values):
            if b == 0:
                first = value[u * ROWS : u * ROWS + CY]
                rest = value[u * ROWS + CY : (u + 1) * ROWS]
            else:
                first = value[u * CY : (u + 1) * CY]
                at = (units + u // 2) * CY
                rest = value[at : at + CY]
                rest = jnp.where(filled, pltpu.roll(rest, CY // 2, 0) if u % 2 else rest, 0.0)
            add(b, first)
            if n_gy == 2:
                add(b + 1, rest)
            else:
                add(b + 1, jnp.where(half, rest, 0.0))
                add(b - 1, jnp.where(half, 0.0, rest))
        exact = jnp.concatenate(blocks, 0)
        value = exact.astype(BF16)
        out_ref[u * wide : (u + 1) * wide, :] = value
        if u < EXT or planes - EXT <= u:
            v = u if u < EXT else u - planes + 2 * EXT
            far_ref[v * wide : (v + 1) * wide, :] = value
            exact_ref[v * wide : (v + 1) * wide, :] = exact


def along_z_taps(parts, row, radius):
    lane = iota((8, 128), 1)
    total = parts[radius, row : row + 8, :128]
    outside = [jnp.zeros((8, 128), F32)] * 3
    for k in range(2 * radius + 1):
        inner = parts[k, row : row + 8, :128]
        outer = parts[k, row : row + 8, 128:]
        step = radius - k
        if step:
            taken = lane >= 128 - step if step > 0 else lane < -step
            total = total + pltpu.roll(jnp.where(taken, outer, inner), step % 128, 1)
        for n, z in enumerate((-1, CZ, CZ + 1)):
            at = z - step
            value = inner if 0 <= at < CZ else outer
            outside[n] = jnp.where(lane == at % 128, value, outside[n])
    return total, [jnp.sum(v, axis=1, keepdims=True) for v in outside]


def rim_of(block, base, p, wide, group_planes):
    g, q = divmod(p, group_planes)
    packed = block[base + q * wide : base + (q + 1) * wide].astype(F32)
    return pltpu.roll(packed, (-g * LANES) % 128, 1) if g else packed


def own_kernel(tiles, group_planes, wide, span, own_ref, band_ref, total_ref, outside_ref, window, parts):
    planes = tiles + EXT
    radius = span // 2
    alone = tiles - EXT
    own = own_ref[...]
    lane = iota((wide, 128), 1)
    rim = (lane < LANES // 2) | (lane >= 128 - LANES // 2)
    for n in range(alone):
        rows = slice(n * wide, (n + 1) * wide)
        p = EXT + n
        window[rows, :128] = own[p * wide : (p + 1) * wide]
        edge = rim_of(own, planes * wide, p, wide, group_planes)
        window[rows, 128:] = jnp.where(rim, edge, 0.0).astype(BF16)
    for x in range(0, planes, AHEAD):
        first = (radius + EXT - x) * wide
        part = jnp.dot(
            band_ref[:, first : first + alone * wide], window[...], preferred_element_type=F32
        )
        at = row_of(x)
        for k in range(span):
            parts[k, at : at + STEP, :] = part[k * STEP : (k + 1) * STEP]
    lane = iota((8, 128), 1)
    for row in range(0, row_of(planes - 1) + TALL, 8):
        total, outside = along_z_taps(parts, row, radius)
        total_ref[row : row + 8, :] = total
        outside_ref[row : row + 8, :] = jnp.where(
            lane == 0, outside[0], jnp.where(lane == 1, outside[1], outside[2])
        )


def row_of(x):
    return x // AHEAD * STEP + x % AHEAD * TALL


def field_kernel(
    tiles, chunks, group_planes, wide, span,
    own_ref, got1_ref, got3_ref, lower_ref, upper_ref, band_ref, total_ref, outside_ref, y_ref,
    charge_ref, offset_ref, cell_ref, potential_ref, force_ref, window, parts, samples,
):
    planes = tiles + EXT
    radius = span // 2
    even = lax.rem(lax.axis_index("gx"), 2) == 0
    got1, got3 = got1_ref[...], got3_ref[...]
    right = jnp.where(even, got1, got3)
    left = jnp.where(even, got3, got1)
    own = own_ref[...]
    margin = planes * wide
    far_base = 2 * EXT * wide
    lane = iota((wide, 128), 1)
    rim = (lane < LANES // 2) | (lane >= 128 - LANES // 2)

    def main(block, p):
        return block[p * wide : (p + 1) * wide].astype(F32)

    def edge(block, p, base=margin):
        return rim_of(block, base, p, wide, group_planes)

    far_low, far_high = lower_ref[...], upper_ref[...]
    start, stop = radius + EXT, radius + tiles
    place = 0
    for x in range(2 * radius + planes):
        if start <= x < stop:
            continue
        terms = []
        if x < planes:
            terms.append((main(left, x), edge(left, x)))
        if 0 <= x - tiles < planes:
            p = x - tiles
            v = p if p < EXT else p - planes + 2 * EXT
            terms.append((main(own, v), edge(own, p, far_base)))
        if 0 <= x - 2 * tiles < planes:
            terms.append((main(right, x - 2 * tiles), edge(right, x - 2 * tiles)))
        if x < EXT:
            terms.append((main(far_low, EXT + x), edge(far_low, planes - EXT + x, far_base)))
        if 0 <= x - 3 * tiles < EXT:
            terms.append((main(far_high, x - 3 * tiles), edge(far_high, x - 3 * tiles, far_base)))
        rows = slice(place * wide, (place + 1) * wide)
        place += 1
        window[rows, :128] = sum(a for a, _ in terms).astype(BF16)
        window[rows, 128:] = jnp.where(
            rim, sum(b for _, b in terms), 0.0
        ).astype(BF16)

    for x in range(0, planes, AHEAD):
        count = min(AHEAD, planes - x)
        used = span + count - 1 - (stop - start)
        part = jnp.dot(
            band_ref[x // AHEAD, :, : used * wide],
            window[x * wide : (x + used) * wide, :],
            preferred_element_type=F32,
        )
        at = row_of(x)
        for k in range(span):
            parts[k, at : at + STEP, :] = part[k * STEP : (k + 1) * STEP]
    lane = iota((8, 128), 1)
    for row in range(0, row_of(planes - 1) + TALL, 8):
        total, outside = along_z_taps(parts, row, radius)
        total = total + total_ref[row : row + 8, :]
        below, above, beyond = (
            v + outside_ref[row : row + 8, n : n + 1] for n, v in enumerate(outside)
        )
        samples[0, row : row + 8, :] = jnp.where(lane == 0, below, pltpu.roll(total, 1, 1))
        samples[1, row : row + 8, :] = total
        samples[2, row : row + 8, :] = jnp.where(lane == CZ - 1, above, pltpu.roll(total, 127, 1))
        samples[3, row : row + 8, :] = jnp.where(
            lane == CZ - 1, beyond, jnp.where(lane == CZ - 2, above, pltpu.roll(total, 126, 1))
        )
    for x in range(tiles):
        potential_ref[x] = samples[1, row_of(x + 1) + 1 : row_of(x + 1) + 1 + CY, :]

    rows_total = tiles * chunks
    per = 8 // chunks
    pairs = tiles // per
    upper_half = [iota((8, 128), 0) >= chunks * h for h in range(per)]
    for p in range(pairs):
        at = pl.ds(p * 8, 8)
        cz = cell_ref[pl.ds(rows_total + p * 8, 8), :] & (CZ - 1)
        zv, zs = spline(offset_ref[pl.ds(2 * rows_total + p * 8, 8), :])
        xv, xs = spline(offset_ref[at, :])
        force = [jnp.zeros((8, 128), F32)] * 3
        for k in range(4):
            plain = [jnp.zeros((8, 128), F32)] * 4
            sloped = [jnp.zeros((8, 128), F32)] * 4
            for y in range(TALL):
                y_at = pl.ds((p * TALL + y) * 8, 8)
                y_value = y_ref[0, y_at, :]
                y_slope = y_ref[1, y_at, :]
                for c in range(4):
                    source = None
                    for h in range(per):
                        row = row_of(p * per + k + h) + y
                        line = jnp.broadcast_to(samples[c, row : row + 1, :], (8, 128))
                        source = line if h == 0 else jnp.where(upper_half[h], line, source)
                    picked = jnp.take_along_axis(source, cz, axis=1)
                    plain[c] = plain[c] + y_value * picked
                    sloped[c] = sloped[c] + y_slope * picked
            value = sum(zv[c] * plain[c] for c in range(4))
            along_y = sum(zv[c] * sloped[c] for c in range(4))
            along_z = sum(zs[c] * plain[c] for c in range(4))
            force[0] = force[0] + xs[k] * value
            force[1] = force[1] + xv[k] * along_y
            force[2] = force[2] + xv[k] * along_z
        charge = charge_ref[at, :]
        for d in range(3):
            force_ref[d, at, :] = -charge * force[d]


def band_kernel(tiles, chunks, wide, kernel_ref, offset_ref, cell_ref, out_ref, other_ref, y_ref, rows_ref):
    rows_total = tiles * chunks
    for p in range(rows_total // 8):
        yv, ys = spline(offset_ref[pl.ds(rows_total + p * 8, 8), :])
        cy = cell_ref[pl.ds(p * 8, 8), :] & (CY - 1)
        for y in range(TALL):
            at = pl.ds((p * TALL + y) * 8, 8)
            y_ref[0, at, :] = pick(y - cy, yv)
            y_ref[1, at, :] = pick(y - cy, ys)
    span = kernel_ref.shape[0]
    radius = span // 2
    columns = out_ref.shape[1]
    base = jnp.zeros((span, columns), F32)
    tap = iota((span, columns), 0)
    column = iota((span, columns), 1)
    for i in range(span):
        place = jnp.where(
            (column >= i * wide) & (column < (i + 1) * wide)
            & (((column - tap + radius) & (wide - 1)) == 0),
            1.0, 0.0,
        ).astype(BF16)
        base = base + lax.dot_general(
            kernel_ref[i], place, (((0,), (0,)), ((), ())), preferred_element_type=F32
        )
    rows_ref[...] = jnp.zeros_like(rows_ref)
    within = column & (wide - 1)
    for y in range(-1, CY + 2):
        shift = y % wide
        moved = base
        if shift:
            moved = jnp.where(
                within >= shift,
                pltpu.roll(base, shift, 1),
                pltpu.roll(base, (shift - wide) % columns, 1),
            )
        for n in range(AHEAD):
            there = pltpu.roll(moved, n * wide, 1) if n else moved
            for tile in range(columns // 128):
                at = pl.ds(n * TALL + y + 1, span, stride=STEP)
                rows_ref[tile, at, :] = there[:, tile * 128 : (tile + 1) * 128]
    alone = (tiles - EXT) * wide
    whole = jnp.concatenate([rows_ref[tile] for tile in range(columns // 128)], 1)
    out_ref[...] = whole.astype(BF16)
    kept = other_ref.shape[2]
    moved = pltpu.roll(whole, columns - alone, 1)[:, :kept]
    lane = iota(moved.shape, 1)
    for n in range(other_ref.shape[0]):
        first = (radius + EXT - n * AHEAD) * wide
        other_ref[n] = jnp.where(lane < first, whole[:, :kept], moved).astype(BF16)


def vmem(n):
    return [pl.BlockSpec(memory_space=pltpu.VMEM)] * n


def local(charges, offsets, cells, kernel):
    n_gx, n_gy, n_gz = (lax.axis_size(axis) for axis in ("gx", "gy", "gz"))
    tiles, slots = charges.shape[0], charges.shape[3]
    span = kernel.shape[0]
    chunks = slots // 128
    rows = tiles * chunks
    planes = tiles + EXT
    group_planes = -(-planes // GROUPS)
    group = group_planes * ROWS
    wide = n_gy * CY
    band_columns = -(-(span + AHEAD - 1) * wide // 128) * 128
    charge = charges.reshape(rows, 128)
    offset = offsets.reshape(3 * rows, 128)
    cell = cells.reshape(2 * rows, 128)

    def shape(*dims, kind=F32):
        return jax.ShapeDtypeStruct(dims, kind)

    near = lambda n: [(i, i ^ 1) for i in range(n)]
    other = lambda n: [(i, (i + 1 if i % 2 else i - 1) % n) for i in range(n)]
    shift = lambda n, s: [(i, (i + s) % n) for i in range(n)]

    z0, z1, s_high, s_low, weights, z_cell = pl.pallas_call(
        functools.partial(edge_kernel, tiles, chunks, group_planes),
        out_shape=(
            shape(group, 128, kind=BF16), shape(group, 128, kind=BF16),
            shape(tiles * 4 * ROWS, slots, kind=BF16), shape(tiles * 4 * ROWS, slots, kind=BF16),
            shape(8, rows, 128), shape(rows, 128, kind=jnp.int32),
        ),
        in_specs=[pl.BlockSpec(memory_space=pltpu.HBM)] * 3,
        out_specs=tuple(vmem(6)),
        scratch_shapes=[
            pltpu.VMEM((rows, 128), F32),
            pltpu.VMEM((3 * rows, 128), F32),
            pltpu.VMEM((2 * rows, 128), jnp.int32),
            pltpu.VMEM((4, rows, 128), F32),
            pltpu.VMEM((4, rows, 128), F32),
            pltpu.VMEM((GROUPS * group, 128), F32),
            pltpu.SemaphoreType.DMA((3,)),
        ],
        compiler_params=pltpu.CompilerParams(vmem_limit_bytes=8 << 20),
        name="edge",
    )(*(pltpu.with_memory_space_constraint(x, pltpu.HBM) for x in (charge, offset, cell)))
    got0 = lax.ppermute(z0, "gz", near(n_gz))
    got1 = lax.ppermute(z1, "gz", other(n_gz))
    main = pl.pallas_call(
        functools.partial(spread_kernel, tiles, chunks),
        out_shape=shape(planes * ROWS, 128),
        in_specs=vmem(4),
        out_specs=vmem(1)[0],
        compiler_params=pltpu.CompilerParams(vmem_limit_bytes=8 << 20),
        cost_estimate=pl.CostEstimate(flops=400_000_000, bytes_accessed=2_000_000, transcendentals=0),
        name="spread",
    )(s_high, s_low, weights, z_cell)
    units = planes + group_planes
    block, sent = pl.pallas_call(
        functools.partial(z_fold_kernel, tiles, group_planes),
        out_shape=(shape(units * ROWS, 128), shape(-(-(units + -(-units // 2)) // 2) * 2 * CY, 128, kind=BF16)),
        in_specs=vmem(5),
        out_specs=tuple(vmem(2)),
        compiler_params=pltpu.CompilerParams(vmem_limit_bytes=4 << 20),
        name="z_fold",
    )(main, z0, z1, got0, got1)
    sources = [block] + [lax.ppermute(sent, "gy", shift(n_gy, -s)) for s in range(1, n_gy)]
    mine, far, exact = pl.pallas_call(
        functools.partial(y_fold_kernel, n_gy, units, tiles),
        out_shape=(
            shape(units * wide, 128, kind=BF16),
            shape((2 * EXT + group_planes) * wide, 128, kind=BF16),
            shape((2 * EXT + group_planes) * wide, 128),
        ),
        in_specs=vmem(n_gy),
        out_specs=tuple(vmem(3)),
        compiler_params=pltpu.CompilerParams(vmem_limit_bytes=4 << 20),
        name="y_fold",
    )(*sources)
    x1 = lax.ppermute(mine, "gx", near(n_gx))
    lower = lax.ppermute(far, "gx", shift(n_gx, 2))
    upper = lower
    if n_gx != 4:
        upper = lax.ppermute(far, "gx", shift(n_gx, -2))
    x3 = lax.ppermute(mine, "gx", other(n_gx))
    other_columns = -(-(span + AHEAD - 1 - (tiles - EXT)) * wide // 128) * 128
    batches = -(-planes // AHEAD)
    band_call = pl.pallas_call(
        functools.partial(band_kernel, tiles, chunks, wide),
        out_shape=(
            shape(span * STEP, band_columns, kind=BF16),
            shape(batches, span * STEP, other_columns, kind=BF16),
            shape(2, rows * TALL, 128),
        ),
        in_specs=vmem(3),
        out_specs=tuple(vmem(3)),
        scratch_shapes=[pltpu.VMEM((band_columns // 128, span * STEP, 128), F32)],
        compiler_params=pltpu.CompilerParams(vmem_limit_bytes=16 << 20),
        cost_estimate=pl.CostEstimate(flops=400_000_000, bytes_accessed=2_000_000, transcendentals=0),
        name="band",
    )
    band, band_other, y_dense = band_call(kernel, offset, cell)
    own_total, own_outside = pl.pallas_call(
        functools.partial(own_kernel, tiles, group_planes, wide, span),
        out_shape=(shape(batches * STEP, 128), shape(batches * STEP, 128)),
        in_specs=vmem(2),
        out_specs=tuple(vmem(2)),
        scratch_shapes=[
            pltpu.VMEM(((tiles - EXT) * wide, 256), BF16),
            pltpu.VMEM((span, batches * STEP, 256), F32),
        ],
        compiler_params=pltpu.CompilerParams(vmem_limit_bytes=12 << 20),
        cost_estimate=pl.CostEstimate(flops=400_000_000, bytes_accessed=2_000_000, transcendentals=0),
        name="own",
    )(mine, band)
    potential, forces = pl.pallas_call(
        functools.partial(field_kernel, tiles, chunks, group_planes, wide, span),
        out_shape=(shape(tiles, CY, CZ), shape(3, rows, 128)),
        in_specs=vmem(12),
        out_specs=tuple(vmem(2)),
        scratch_shapes=[
            pltpu.VMEM(((2 * (span // 2) + planes) * wide, 256), BF16),
            pltpu.VMEM((span, -(-planes // AHEAD) * STEP, 256), F32),
            pltpu.VMEM((4, -(-planes // AHEAD) * STEP, 128), F32),
        ],
        compiler_params=pltpu.CompilerParams(vmem_limit_bytes=16 << 20),
        name="field",
    )(exact, x1, x3, lower, upper, band_other, own_total, own_outside, y_dense, charge, offset, cell)
    return potential, forces.reshape(3, tiles, 1, 1, slots)


def solution(mesh):
    placed = (
        P("gx", "gy", "gz", None),
        P(None, "gx", "gy", "gz", None),
        P(None, "gx", "gy", "gz", None),
        P(),
    )
    return jax.shard_map(
        local,
        mesh=mesh,
        in_specs=placed,
        out_specs=(P("gx", "gy", "gz"), P(None, "gx", "gy", "gz", None)),
        check_vma=False,
    )
```

```python
import functools

import jax
import jax.numpy as jnp
from jax import lax
from jax.experimental import pallas as pl
from jax.experimental.pallas import tpu as pltpu
from jax.sharding import PartitionSpec as P


CY = 8
CZ = 128
EXT = 3
ROWS = 16
TALL = CY + EXT
AHEAD = 4
STEP = -(-AHEAD * TALL // 8) * 8
LANES = 32
GROUPS = 128 // LANES

F32 = jnp.float32
BF16 = jnp.bfloat16


def spline(fraction):
    remain = 1.0 - fraction
    values = [
        remain**3 / 6.0,
        (3.0 * fraction**3 - 6.0 * fraction**2 + 4.0) / 6.0,
        (-3.0 * fraction**3 + 3.0 * fraction**2 + 3.0 * fraction + 1.0) / 6.0,
        fraction**3 / 6.0,
    ]
    slopes = [
        -0.5 * remain**2,
        1.5 * fraction**2 - 2.0 * fraction,
        -1.5 * fraction**2 + fraction + 0.5,
        0.5 * fraction**2,
    ]
    return values, slopes


def pick(distance, four):
    out = jnp.zeros((), F32)
    for c in reversed(range(4)):
        out = jnp.where(distance == c, four[c], out)
    return out


def split(x):
    high = x.astype(BF16)
    return high, (x - high.astype(F32)).astype(BF16)


def nt_dot(a, b):
    return lax.dot_general(a, b, (((1,), (1,)), ((), ())), preferred_element_type=F32)


def iota(shape, dim, kind=jnp.int32):
    return lax.broadcasted_iota(kind, shape, dim)


def tall(row, kind, count):
    tile = jnp.broadcast_to(row, (16, 128)).astype(kind)
    return jnp.concatenate([tile] * (count // 16), 0)


def z_weights(z_of_row, cell, rows):
    count = z_of_row.shape[0]
    high = low = jnp.zeros((count, 128), BF16)
    for c in range(4):
        here = z_of_row == tall(cell + (c - 1), jnp.int16, count)
        high = jnp.where(here, tall(rows[c], BF16, count), high)
        low = jnp.where(here, tall(rows[4 + c], BF16, count), low)
    return high, low


def edge_kernel(
    tiles, chunks, group_planes, charge_hbm, offset_hbm, cell_hbm, kernel_hbm,
    z0_ref, z1_ref, high_ref, low_ref, weight_ref, cell_ref,
    charge_in, offset_in, cell_in, kernel_in, x_rows, y_rows, acc, sems,
):
    copies = [
        pltpu.make_async_copy(source, target, sems.at[n])
        for n, (source, target) in enumerate(
            (
                (charge_hbm, charge_in),
                (offset_hbm, offset_in),
                (cell_hbm, cell_in),
                (kernel_hbm, kernel_in),
            )
        )
    ]
    for copy in copies:
        copy.start()
    rows = tiles * chunks
    acc[...] = jnp.zeros_like(acc)
    row = iota((LANES, 128), 0, jnp.int16)
    z_of_row = jnp.where(row < LANES // 2, row - 1, row + (CZ + 2 - LANES // 2 - 11))
    y_row = iota((ROWS, 128), 0)
    y_of_row = jnp.where(y_row < 12, y_row, y_row - ROWS)
    for copy in copies[:3]:
        copy.wait()
    for r in range(0, rows, 8):
        at = pl.ds(r, 8)
        xv, _ = spline(offset_in[at, :])
        yv, _ = spline(offset_in[pl.ds(rows + r, 8), :])
        zv, _ = spline(offset_in[pl.ds(2 * rows + r, 8), :])
        charge = charge_in[at, :]
        for c in range(4):
            x_rows[c, at, :] = charge * xv[c]
            y_rows[c, at, :] = yv[c]
            high = zv[c].astype(BF16).astype(F32)
            weight_ref[c, at, :] = high
            weight_ref[4 + c, at, :] = zv[c] - high
        cell_ref[at, :] = cell_in[pl.ds(rows + r, 8), :] & (CZ - 1)
    for t in range(tiles):
        parts = [], [], [], []
        for j in range(chunks):
            at = pl.ds(t * chunks + j, 1)
            cy = cell_in[at, :] & (CY - 1)
            y_dense = pick(y_of_row - (cy - 1), [y_rows[c, at, :] for c in range(4)])
            s = jnp.concatenate([y_dense * x_rows[k, at, :] for k in range(4)], 0)
            z = z_weights(z_of_row, cell_ref[at, :], [weight_ref[c, at, :] for c in range(8)])
            for part, value in zip(parts, split(s) + z):
                part.append(value)
        s_high, s_low, z_high, z_low = (jnp.concatenate(part, 1) for part in parts)
        high_ref[t * 4 * ROWS : (t + 1) * 4 * ROWS, :] = s_high
        low_ref[t * 4 * ROWS : (t + 1) * 4 * ROWS, :] = s_low
        both = nt_dot(jnp.concatenate([s_high, s_low], 0), z_high)
        got = both[: 4 * ROWS] + both[4 * ROWS :] + nt_dot(s_high, z_low)
        acc[t * ROWS : (t + 4) * ROWS, :LANES] += got
    group = group_planes * ROWS
    lane = iota((group, 128), 1)
    lower_out = jnp.zeros((group, 128), F32)
    upper_out = jnp.zeros((group, 128), F32)
    for g in range(GROUPS):
        edge = acc[g * group : (g + 1) * group, :]
        low = jnp.where(lane < LANES // 2, edge, 0.0)
        high = jnp.where(lane >= LANES // 2, edge, 0.0)
        lower_out = lower_out + pltpu.roll(low, (g * LANES - 1) % 128, 1)
        upper_out = upper_out + pltpu.roll(high, (g * LANES - LANES // 2 - 9) % 128, 1)
    even = lax.rem(lax.axis_index("gz"), 2) == 0
    z0_ref[...] = jnp.where(even, upper_out, lower_out).astype(BF16)
    z1_ref[...] = jnp.where(even, lower_out, upper_out).astype(BF16)
    copies[3].wait()


def spread_kernel(tiles, chunks, high_ref, low_ref, weight_ref, cell_ref, main_ref):
    main_ref[...] = jnp.zeros_like(main_ref)
    z_of_row = iota((CZ, 128), 0, jnp.int16)
    for t in range(tiles):
        parts = [], []
        for j in range(chunks):
            at = pl.ds(t * chunks + j, 1)
            z = z_weights(z_of_row, cell_ref[at, :], [weight_ref[c, at, :] for c in range(8)])
            for part, value in zip(parts, z):
                part.append(value)
        z_high, z_low = (jnp.concatenate(part, 1) for part in parts)
        s_high = high_ref[t * 4 * ROWS : (t + 1) * 4 * ROWS, :]
        s_low = low_ref[t * 4 * ROWS : (t + 1) * 4 * ROWS, :]
        both = nt_dot(jnp.concatenate([s_high, s_low], 0), z_high)
        got = both[: 4 * ROWS] + both[4 * ROWS :] + nt_dot(s_high, z_low)
        main_ref[t * ROWS : (t + 4) * ROWS, :] += got


def z_fold_kernel(tiles, group_planes, main_ref, z0_ref, z1_ref, got0_ref, got1_ref, out_ref, sent_ref):
    planes = tiles + EXT
    group = group_planes * ROWS
    units = []
    even = lax.rem(lax.axis_index("gz"), 2) == 0
    z0, z1, got0, got1 = (ref[...].astype(F32) for ref in (z0_ref, z1_ref, got0_ref, got1_ref))
    own_upper = jnp.where(even, z0, z1)
    own_lower = jnp.where(even, z1, z0)
    right_lower = jnp.where(even, got0, got1)
    left_upper = jnp.where(even, got1, got0)
    lane = iota((group, 128), 1)
    first = ((lane + LANES // 2) & (LANES - 1)) >= LANES // 2
    rim = (lane < LANES // 2) | (lane >= 128 - LANES // 2)
    halo = jnp.where(first, right_lower + own_upper, left_upper + own_lower)
    inner = jnp.where(first, left_upper, right_lower)
    for g in range(GROUPS):
        count = min(group, planes * ROWS - g * group)
        add = jnp.where(rim, pltpu.roll(inner, (-g * LANES) % 128, 1) if g else inner, 0.0)
        total = main_ref[g * group : g * group + count, :] + add[:count]
        out_ref[g * group : g * group + count, :] = total
        units += [total[at : at + ROWS] for at in range(0, count, ROWS)]
    out_ref[planes * ROWS : planes * ROWS + group, :] = halo
    units += [halo[at : at + ROWS] for at in range(0, group, ROWS)]
    inner = [unit[:CY] for unit in units]
    outer = [unit[CY:] for unit in units]
    outer = [
        pair[0] + pltpu.roll(pair[1], CY // 2, 0) if len(pair) > 1 else pair[0]
        for pair in (outer[u : u + 2] for u in range(0, len(outer), 2))
    ]
    halves = inner + outer
    halves += [jnp.zeros((CY, 128), F32)] * (len(halves) % 2)
    for u in range(0, len(halves), 2):
        sent_ref[u * CY : (u + 2) * CY, :] = jnp.concatenate(halves[u : u + 2], 0).astype(BF16)


def y_fold_kernel(n_gy, units, tiles, *refs):
    sources, (out_ref, far_ref, exact_ref) = refs[:n_gy], refs[n_gy:]
    half = iota((CY, 128), 0) < CY // 2
    filled = (iota((CY, 128), 0) < 2) | (iota((CY, 128), 0) == CY - 1)
    values = [ref[...].astype(F32) for ref in sources]
    wide = n_gy * CY
    planes = tiles + EXT
    for u in range(units):
        blocks = [None] * n_gy

        def add(b, value):
            b = b % n_gy
            blocks[b] = value if blocks[b] is None else blocks[b] + value

        for b, value in enumerate(values):
            if b == 0:
                first = value[u * ROWS : u * ROWS + CY]
                rest = value[u * ROWS + CY : (u + 1) * ROWS]
            else:
                first = value[u * CY : (u + 1) * CY]
                at = (units + u // 2) * CY
                rest = value[at : at + CY]
                rest = jnp.where(filled, pltpu.roll(rest, CY // 2, 0) if u % 2 else rest, 0.0)
            add(b, first)
            if n_gy == 2:
                add(b + 1, rest)
            else:
                add(b + 1, jnp.where(half, rest, 0.0))
                add(b - 1, jnp.where(half, 0.0, rest))
        exact = jnp.concatenate(blocks, 0)
        value = exact.astype(BF16)
        out_ref[u * wide : (u + 1) * wide, :] = value
        if u < EXT or planes - EXT <= u:
            v = u if u < EXT else u - planes + 2 * EXT
            far_ref[v * wide : (v + 1) * wide, :] = value
            exact_ref[v * wide : (v + 1) * wide, :] = exact


def along_z_taps(parts, row, radius):
    lane = iota((8, 128), 1)
    total = parts[radius, row : row + 8, :128]
    outside = [jnp.zeros((8, 128), F32)] * 3
    for k in range(2 * radius + 1):
        inner = parts[k, row : row + 8, :128]
        outer = parts[k, row : row + 8, 128:]
        step = radius - k
        if step:
            taken = lane >= 128 - step if step > 0 else lane < -step
            total = total + pltpu.roll(jnp.where(taken, outer, inner), step % 128, 1)
        for n, z in enumerate((-1, CZ, CZ + 1)):
            at = z - step
            value = inner if 0 <= at < CZ else outer
            outside[n] = jnp.where(lane == at % 128, value, outside[n])
    return total, [jnp.sum(v, axis=1, keepdims=True) for v in outside]


def rim_of(block, base, p, wide, group_planes):
    g, q = divmod(p, group_planes)
    packed = block[base + q * wide : base + (q + 1) * wide].astype(F32)
    return pltpu.roll(packed, (-g * LANES) % 128, 1) if g else packed


def own_kernel(tiles, group_planes, wide, span, own_ref, band_ref, total_ref, outside_ref, window, parts):
    planes = tiles + EXT
    radius = span // 2
    alone = tiles - EXT
    own = own_ref[...]
    lane = iota((wide, 128), 1)
    rim = (lane < LANES // 2) | (lane >= 128 - LANES // 2)
    for n in range(alone):
        rows = slice(n * wide, (n + 1) * wide)
        p = EXT + n
        window[rows, :128] = own[p * wide : (p + 1) * wide]
        edge = rim_of(own, planes * wide, p, wide, group_planes)
        window[rows, 128:] = jnp.where(rim, edge, 0.0).astype(BF16)
    for x in range(0, planes, AHEAD):
        first = (radius + EXT - x) * wide
        part = jnp.dot(
            band_ref[:, first : first + alone * wide], window[...], preferred_element_type=F32
        )
        at = row_of(x)
        for k in range(span):
            parts[k, at : at + STEP, :] = part[k * STEP : (k + 1) * STEP]
    lane = iota((8, 128), 1)
    for row in range(0, row_of(planes - 1) + TALL, 8):
        total, outside = along_z_taps(parts, row, radius)
        total_ref[row : row + 8, :] = total
        outside_ref[row : row + 8, :] = jnp.where(
            lane == 0, outside[0], jnp.where(lane == 1, outside[1], outside[2])
        )


def row_of(x):
    return x // AHEAD * STEP + x % AHEAD * TALL


def field_kernel(
    tiles, chunks, group_planes, wide, span,
    own_ref, got1_ref, got3_ref, lower_ref, upper_ref, band_ref, total_ref, outside_ref,
    hot_ref, weight_ref, z_ref, potential_ref, force_ref, window, parts, samples,
):
    planes = tiles + EXT
    radius = span // 2
    even = lax.rem(lax.axis_index("gx"), 2) == 0
    got1, got3 = got1_ref[...], got3_ref[...]
    right = jnp.where(even, got1, got3)
    left = jnp.where(even, got3, got1)
    own = own_ref[...]
    margin = planes * wide
    far_base = 2 * EXT * wide
    lane = iota((wide, 128), 1)
    rim = (lane < LANES // 2) | (lane >= 128 - LANES // 2)

    def main(block, p):
        return block[p * wide : (p + 1) * wide].astype(F32)

    def edge(block, p, base=margin):
        return rim_of(block, base, p, wide, group_planes)

    far_low, far_high = lower_ref[...], upper_ref[...]
    start, stop = radius + EXT, radius + tiles
    place = 0
    for x in range(2 * radius + planes):
        if start <= x < stop:
            continue
        terms = []
        if x < planes:
            terms.append((main(left, x), edge(left, x)))
        if 0 <= x - tiles < planes:
            p = x - tiles
            v = p if p < EXT else p - planes + 2 * EXT
            terms.append((main(own, v), edge(own, p, far_base)))
        if 0 <= x - 2 * tiles < planes:
            terms.append((main(right, x - 2 * tiles), edge(right, x - 2 * tiles)))
        if x < EXT:
            terms.append((main(far_low, EXT + x), edge(far_low, planes - EXT + x, far_base)))
        if 0 <= x - 3 * tiles < EXT:
            terms.append((main(far_high, x - 3 * tiles), edge(far_high, x - 3 * tiles, far_base)))
        rows = slice(place * wide, (place + 1) * wide)
        place += 1
        window[rows, :128] = sum(a for a, _ in terms).astype(BF16)
        window[rows, 128:] = jnp.where(
            rim, sum(b for _, b in terms), 0.0
        ).astype(BF16)

    for x in range(0, planes, AHEAD):
        count = min(AHEAD, planes - x)
        used = span + count - 1 - (stop - start)
        part = jnp.dot(
            band_ref[x // AHEAD, :, : used * wide],
            window[x * wide : (x + used) * wide, :],
            preferred_element_type=F32,
        )
        at = row_of(x)
        for k in range(span):
            parts[k, at : at + STEP, :] = part[k * STEP : (k + 1) * STEP]
    lane = iota((8, 128), 1)
    for row in range(0, row_of(planes - 1) + TALL, 8):
        total, outside = along_z_taps(parts, row, radius)
        total = total + total_ref[row : row + 8, :]
        below, above, beyond = (
            v + outside_ref[row : row + 8, n : n + 1] for n, v in enumerate(outside)
        )
        samples[0, row : row + 8, :] = jnp.where(lane == 0, below, pltpu.roll(total, 1, 1))
        samples[1, row : row + 8, :] = total
        samples[2, row : row + 8, :] = jnp.where(lane == CZ - 1, above, pltpu.roll(total, 127, 1))
        samples[3, row : row + 8, :] = jnp.where(
            lane == CZ - 1, beyond, jnp.where(lane == CZ - 2, above, pltpu.roll(total, 126, 1))
        )
    for x in range(tiles):
        potential_ref[x] = samples[1, row_of(x + 1) + 1 : row_of(x + 1) + 1 + CY, :]

    for t in range(tiles):
        rows = slice(row_of(t), row_of(t) + STEP)
        halves = [jnp.concatenate(split(samples[c, rows, :]), 1) for c in range(4)]
        picked = jnp.dot(jnp.concatenate(halves, 0), hot_ref[t], preferred_element_type=F32)
        for j in range(chunks):
            at = t * chunks + j
            lanes = slice(j * 128, (j + 1) * 128)
            four = [picked[c * STEP : (c + 1) * STEP, lanes] for c in range(4)]
            value = sum(z_ref[c, at : at + 1, :] * four[c] for c in range(4))
            slope = sum(z_ref[4 + c, at : at + 1, :] * four[c] for c in range(4))
            for d, part in enumerate((value, value, slope)):
                force_ref[d, at : at + 1, :] = jnp.sum(
                    weight_ref[t, d, :, lanes] * part, axis=0, keepdims=True
                )


def weight_kernel(tiles, chunks, charge_ref, offset_ref, cell_ref, hot_ref, weight_ref, z_ref, x_rows, y_rows):
    rows = tiles * chunks
    for r in range(0, rows, 8):
        at = pl.ds(r, 8)
        charge = charge_ref[at, :]
        xs = spline(offset_ref[at, :])
        ys = spline(offset_ref[pl.ds(rows + r, 8), :])
        zs = spline(offset_ref[pl.ds(2 * rows + r, 8), :])
        for w in range(2):
            for c in range(4):
                x_rows[4 * w + c, at, :] = -charge * xs[w][c]
                y_rows[4 * w + c, at, :] = ys[w][c]
                z_ref[4 * w + c, at, :] = zs[w][c]
    z_of_row = iota((CZ, 128), 0, jnp.int16)
    one, zero = jnp.ones((CZ, 128), BF16), jnp.zeros((CZ, 128), BF16)
    row = iota((STEP, 128), 0)
    for t in range(tiles):
        starts = [row_of(t + k) - row_of(t) for k in range(4)]
        plane = [row >= start for start in starts]
        y_of_row = row - sum(
            jnp.where(plane[k], starts[k] - starts[k - 1], 0) for k in range(1, 4)
        )
        for j in range(chunks):
            at = pl.ds(t * chunks + j, 1)
            lanes = slice(j * 128, (j + 1) * 128)
            cy = cell_ref[at, :] & (CY - 1)
            cz = cell_ref[pl.ds(rows + t * chunks + j, 1), :] & (CZ - 1)
            hot = jnp.where(z_of_row == tall(cz, jnp.int16, CZ), one, zero)
            hot_ref[t, :CZ, lanes] = hot
            hot_ref[t, CZ:, lanes] = hot
            gap = y_of_row - cy
            here = [gap == c for c in range(4)]

            def line(ref, n):
                return ref[n, at, :]

            y_value = y_slope = jnp.zeros((STEP, 128), F32)
            for c in range(4):
                y_value = jnp.where(here[c], line(y_rows, c), y_value)
                y_slope = jnp.where(here[c], line(y_rows, 4 + c), y_slope)
            x_value = x_slope = jnp.zeros((STEP, 128), F32)
            for k in range(4):
                x_value = jnp.where(plane[k], line(x_rows, k), x_value)
                x_slope = jnp.where(plane[k], line(x_rows, 4 + k), x_slope)
            weight_ref[t, 0, :, lanes] = x_slope * y_value
            weight_ref[t, 1, :, lanes] = x_value * y_slope
            weight_ref[t, 2, :, lanes] = x_value * y_value


def band_kernel(tiles, wide, kernel_ref, out_ref, other_ref, rows_ref):
    span = kernel_ref.shape[0]
    radius = span // 2
    columns = out_ref.shape[1]
    base = jnp.zeros((span, columns), F32)
    tap = iota((span, columns), 0)
    column = iota((span, columns), 1)
    for i in range(span):
        place = jnp.where(
            (column >= i * wide) & (column < (i + 1) * wide)
            & (((column - tap + radius) & (wide - 1)) == 0),
            1.0, 0.0,
        ).astype(BF16)
        base = base + lax.dot_general(
            kernel_ref[i], place, (((0,), (0,)), ((), ())), preferred_element_type=F32
        )
    rows_ref[...] = jnp.zeros_like(rows_ref)
    within = column & (wide - 1)
    for y in range(-1, CY + 2):
        shift = y % wide
        moved = base
        if shift:
            moved = jnp.where(
                within >= shift,
                pltpu.roll(base, shift, 1),
                pltpu.roll(base, (shift - wide) % columns, 1),
            )
        for n in range(AHEAD):
            there = pltpu.roll(moved, n * wide, 1) if n else moved
            for tile in range(columns // 128):
                at = pl.ds(n * TALL + y + 1, span, stride=STEP)
                rows_ref[tile, at, :] = there[:, tile * 128 : (tile + 1) * 128]
    alone = (tiles - EXT) * wide
    whole = jnp.concatenate([rows_ref[tile] for tile in range(columns // 128)], 1)
    out_ref[...] = whole.astype(BF16)
    kept = other_ref.shape[2]
    moved = pltpu.roll(whole, columns - alone, 1)[:, :kept]
    lane = iota(moved.shape, 1)
    for n in range(other_ref.shape[0]):
        first = (radius + EXT - n * AHEAD) * wide
        other_ref[n] = jnp.where(lane < first, whole[:, :kept], moved).astype(BF16)


def vmem(n):
    return [pl.BlockSpec(memory_space=pltpu.VMEM)] * n


def local(charges, offsets, cells, kernel):
    n_gx, n_gy, n_gz = (lax.axis_size(axis) for axis in ("gx", "gy", "gz"))
    tiles, slots = charges.shape[0], charges.shape[3]
    span = kernel.shape[0]
    chunks = slots // 128
    rows = tiles * chunks
    planes = tiles + EXT
    group_planes = -(-planes // GROUPS)
    group = group_planes * ROWS
    wide = n_gy * CY
    band_columns = -(-(span + AHEAD - 1) * wide // 128) * 128
    charge = charges.reshape(rows, 128)
    offset = offsets.reshape(3 * rows, 128)
    cell = cells.reshape(2 * rows, 128)

    def shape(*dims, kind=F32):
        return jax.ShapeDtypeStruct(dims, kind)

    near = lambda n: [(i, i ^ 1) for i in range(n)]
    other = lambda n: [(i, (i + 1 if i % 2 else i - 1) % n) for i in range(n)]
    shift = lambda n, s: [(i, (i + s) % n) for i in range(n)]

    z0, z1, s_high, s_low, weights, z_cell, charge_in, offset_in, cell_in, kernel_in = pl.pallas_call(
        functools.partial(edge_kernel, tiles, chunks, group_planes),
        out_shape=(
            shape(group, 128, kind=BF16), shape(group, 128, kind=BF16),
            shape(tiles * 4 * ROWS, slots, kind=BF16), shape(tiles * 4 * ROWS, slots, kind=BF16),
            shape(8, rows, 128), shape(rows, 128, kind=jnp.int32),
            shape(rows, 128), shape(3 * rows, 128), shape(2 * rows, 128, kind=jnp.int32),
            shape(*kernel.shape, kind=kernel.dtype),
        ),
        in_specs=[pl.BlockSpec(memory_space=pltpu.HBM)] * 4,
        out_specs=tuple(vmem(10)),
        scratch_shapes=[
            pltpu.VMEM((4, rows, 128), F32),
            pltpu.VMEM((4, rows, 128), F32),
            pltpu.VMEM((GROUPS * group, 128), F32),
            pltpu.SemaphoreType.DMA((4,)),
        ],
        compiler_params=pltpu.CompilerParams(vmem_limit_bytes=8 << 20),
        name="edge",
    )(*(pltpu.with_memory_space_constraint(x, pltpu.HBM) for x in (charge, offset, cell, kernel)))
    got0 = lax.ppermute(z0, "gz", near(n_gz))
    got1 = lax.ppermute(z1, "gz", other(n_gz))
    main = pl.pallas_call(
        functools.partial(spread_kernel, tiles, chunks),
        out_shape=shape(planes * ROWS, 128),
        in_specs=vmem(4),
        out_specs=vmem(1)[0],
        compiler_params=pltpu.CompilerParams(vmem_limit_bytes=8 << 20),
        cost_estimate=pl.CostEstimate(flops=400_000_000, bytes_accessed=2_000_000, transcendentals=0),
        name="spread",
    )(s_high, s_low, weights, z_cell)
    units = planes + group_planes
    block, sent = pl.pallas_call(
        functools.partial(z_fold_kernel, tiles, group_planes),
        out_shape=(shape(units * ROWS, 128), shape(-(-(units + -(-units // 2)) // 2) * 2 * CY, 128, kind=BF16)),
        in_specs=vmem(5),
        out_specs=tuple(vmem(2)),
        compiler_params=pltpu.CompilerParams(vmem_limit_bytes=4 << 20),
        name="z_fold",
    )(main, z0, z1, got0, got1)
    sources = [block] + [lax.ppermute(sent, "gy", shift(n_gy, -s)) for s in range(1, n_gy)]
    mine, far, exact = pl.pallas_call(
        functools.partial(y_fold_kernel, n_gy, units, tiles),
        out_shape=(
            shape(units * wide, 128, kind=BF16),
            shape((2 * EXT + group_planes) * wide, 128, kind=BF16),
            shape((2 * EXT + group_planes) * wide, 128),
        ),
        in_specs=vmem(n_gy),
        out_specs=tuple(vmem(3)),
        compiler_params=pltpu.CompilerParams(vmem_limit_bytes=4 << 20),
        name="y_fold",
    )(*sources)
    x1 = lax.ppermute(mine, "gx", near(n_gx))
    lower = lax.ppermute(far, "gx", shift(n_gx, 2))
    upper = lower
    if n_gx != 4:
        upper = lax.ppermute(far, "gx", shift(n_gx, -2))
    x3 = lax.ppermute(mine, "gx", other(n_gx))
    other_columns = -(-(span + AHEAD - 1 - (tiles - EXT)) * wide // 128) * 128
    batches = -(-planes // AHEAD)
    band_call = pl.pallas_call(
        functools.partial(band_kernel, tiles, wide),
        out_shape=(
            shape(span * STEP, band_columns, kind=BF16),
            shape(batches, span * STEP, other_columns, kind=BF16),
        ),
        in_specs=vmem(1),
        out_specs=tuple(vmem(2)),
        scratch_shapes=[pltpu.VMEM((band_columns // 128, span * STEP, 128), F32)],
        compiler_params=pltpu.CompilerParams(vmem_limit_bytes=16 << 20),
        cost_estimate=pl.CostEstimate(flops=400_000_000, bytes_accessed=2_000_000, transcendentals=0),
        name="band",
    )
    band, band_other = band_call(kernel_in)
    hot, weights_xy, weights_z = pl.pallas_call(
        functools.partial(weight_kernel, tiles, chunks),
        out_shape=(
            shape(tiles, 2 * CZ, slots, kind=BF16),
            shape(tiles, 3, STEP, slots),
            shape(8, rows, 128),
        ),
        in_specs=vmem(3),
        out_specs=tuple(vmem(3)),
        scratch_shapes=[pltpu.VMEM((8, rows, 128), F32), pltpu.VMEM((8, rows, 128), F32)],
        compiler_params=pltpu.CompilerParams(vmem_limit_bytes=12 << 20),
        cost_estimate=pl.CostEstimate(flops=400_000_000, bytes_accessed=2_000_000, transcendentals=0),
        name="weights",
    )(charge_in, offset_in, cell_in)
    own_total, own_outside = pl.pallas_call(
        functools.partial(own_kernel, tiles, group_planes, wide, span),
        out_shape=(shape(batches * STEP, 128), shape(batches * STEP, 128)),
        in_specs=vmem(2),
        out_specs=tuple(vmem(2)),
        scratch_shapes=[
            pltpu.VMEM(((tiles - EXT) * wide, 256), BF16),
            pltpu.VMEM((span, batches * STEP, 256), F32),
        ],
        compiler_params=pltpu.CompilerParams(vmem_limit_bytes=12 << 20),
        cost_estimate=pl.CostEstimate(flops=400_000_000, bytes_accessed=2_000_000, transcendentals=0),
        name="own",
    )(mine, band)
    potential, forces = pl.pallas_call(
        functools.partial(field_kernel, tiles, chunks, group_planes, wide, span),
        out_shape=(shape(tiles, CY, CZ), shape(3, rows, 128)),
        in_specs=vmem(11),
        out_specs=tuple(vmem(2)),
        scratch_shapes=[
            pltpu.VMEM(((2 * (span // 2) + planes) * wide, 256), BF16),
            pltpu.VMEM((span, -(-planes // AHEAD) * STEP, 256), F32),
            pltpu.VMEM((4, -(-planes // AHEAD) * STEP, 128), F32),
        ],
        compiler_params=pltpu.CompilerParams(vmem_limit_bytes=16 << 20),
        name="field",
    )(exact, x1, x3, lower, upper, band_other, own_total, own_outside, hot, weights_xy, weights_z)
    return potential, forces.reshape(3, tiles, 1, 1, slots)


def solution(mesh):
    placed = (
        P("gx", "gy", "gz", None),
        P(None, "gx", "gy", "gz", None),
        P(None, "gx", "gy", "gz", None),
        P(),
    )
    return jax.shard_map(
        local,
        mesh=mesh,
        in_specs=placed,
        out_specs=(P("gx", "gy", "gz"), P(None, "gx", "gy", "gz", None)),
        check_vma=False,
    )
```

```python
import functools

import jax
import jax.numpy as jnp
from jax import lax
from jax.experimental import pallas as pl
from jax.experimental.pallas import tpu as pltpu
from jax.sharding import PartitionSpec as P


CY = 8
CZ = 128
EXT = 3
ROWS = 16
TALL = CY + EXT
AHEAD = 4
STEP = -(-AHEAD * TALL // 8) * 8
LANES = 32
GROUPS = 128 // LANES

F32 = jnp.float32
BF16 = jnp.bfloat16


def spline(fraction):
    remain = 1.0 - fraction
    values = [
        remain**3 / 6.0,
        (3.0 * fraction**3 - 6.0 * fraction**2 + 4.0) / 6.0,
        (-3.0 * fraction**3 + 3.0 * fraction**2 + 3.0 * fraction + 1.0) / 6.0,
        fraction**3 / 6.0,
    ]
    slopes = [
        -0.5 * remain**2,
        1.5 * fraction**2 - 2.0 * fraction,
        -1.5 * fraction**2 + fraction + 0.5,
        0.5 * fraction**2,
    ]
    return values, slopes


def pick(distance, four):
    out = jnp.zeros((), F32)
    for c in reversed(range(4)):
        out = jnp.where(distance == c, four[c], out)
    return out


def split(x):
    high = x.astype(BF16)
    return high, (x - high.astype(F32)).astype(BF16)


def nt_dot(a, b):
    return lax.dot_general(a, b, (((1,), (1,)), ((), ())), preferred_element_type=F32)


def iota(shape, dim, kind=jnp.int32):
    return lax.broadcasted_iota(kind, shape, dim)


def tall(row, kind, count):
    tile = jnp.broadcast_to(row, (16, 128)).astype(kind)
    return jnp.concatenate([tile] * (count // 16), 0)


def z_weights(z_of_row, cell, rows):
    count = z_of_row.shape[0]
    high = low = jnp.zeros((count, 128), BF16)
    for c in range(4):
        here = z_of_row == tall(cell + (c - 1), jnp.int16, count)
        high = jnp.where(here, tall(rows[c], BF16, count), high)
        low = jnp.where(here, tall(rows[4 + c], BF16, count), low)
    return high, low


def edge_kernel(
    tiles, chunks, group_planes, charge_hbm, offset_hbm, cell_hbm, kernel_hbm,
    z0_ref, z1_ref, high_ref, low_ref, weight_ref, cell_ref,
    charge_in, offset_in, cell_in, kernel_in, x_rows, y_rows, acc, sems,
):
    copies = [
        pltpu.make_async_copy(source, target, sems.at[n])
        for n, (source, target) in enumerate(
            (
                (charge_hbm, charge_in),
                (offset_hbm, offset_in),
                (cell_hbm, cell_in),
                (kernel_hbm, kernel_in),
            )
        )
    ]
    for copy in copies:
        copy.start()
    rows = tiles * chunks
    acc[...] = jnp.zeros_like(acc)
    row = iota((LANES, 128), 0, jnp.int16)
    z_of_row = jnp.where(row < LANES // 2, row - 1, row + (CZ + 2 - LANES // 2 - 11))
    y_row = iota((ROWS, 128), 0)
    y_of_row = jnp.where(y_row < 12, y_row, y_row - ROWS)
    for copy in copies[:3]:
        copy.wait()
    for r in range(0, rows, 8):
        at = pl.ds(r, 8)
        xv, _ = spline(offset_in[at, :])
        yv, _ = spline(offset_in[pl.ds(rows + r, 8), :])
        zv, _ = spline(offset_in[pl.ds(2 * rows + r, 8), :])
        charge = charge_in[at, :]
        for c in range(4):
            x_rows[c, at, :] = charge * xv[c]
            y_rows[c, at, :] = yv[c]
            high = zv[c].astype(BF16).astype(F32)
            weight_ref[c, at, :] = high
            weight_ref[4 + c, at, :] = zv[c] - high
        cell_ref[at, :] = cell_in[pl.ds(rows + r, 8), :] & (CZ - 1)
    for t in range(tiles):
        parts = [], [], [], []
        for j in range(chunks):
            at = pl.ds(t * chunks + j, 1)
            cy = cell_in[at, :] & (CY - 1)
            y_dense = pick(y_of_row - (cy - 1), [y_rows[c, at, :] for c in range(4)])
            s = jnp.concatenate([y_dense * x_rows[k, at, :] for k in range(4)], 0)
            z = z_weights(z_of_row, cell_ref[at, :], [weight_ref[c, at, :] for c in range(8)])
            for part, value in zip(parts, split(s) + z):
                part.append(value)
        s_high, s_low, z_high, z_low = (jnp.concatenate(part, 1) for part in parts)
        high_ref[t * 4 * ROWS : (t + 1) * 4 * ROWS, :] = s_high
        low_ref[t * 4 * ROWS : (t + 1) * 4 * ROWS, :] = s_low
        both = nt_dot(jnp.concatenate([s_high, s_low], 0), z_high)
        got = both[: 4 * ROWS] + both[4 * ROWS :] + nt_dot(s_high, z_low)
        acc[t * ROWS : (t + 4) * ROWS, :LANES] += got
    group = group_planes * ROWS
    lane = iota((group, 128), 1)
    lower_out = jnp.zeros((group, 128), F32)
    upper_out = jnp.zeros((group, 128), F32)
    for g in range(GROUPS):
        edge = acc[g * group : (g + 1) * group, :]
        low = jnp.where(lane < LANES // 2, edge, 0.0)
        high = jnp.where(lane >= LANES // 2, edge, 0.0)
        lower_out = lower_out + pltpu.roll(low, (g * LANES - 1) % 128, 1)
        upper_out = upper_out + pltpu.roll(high, (g * LANES - LANES // 2 - 9) % 128, 1)
    even = lax.rem(lax.axis_index("gz"), 2) == 0
    z0_ref[...] = jnp.where(even, upper_out, lower_out).astype(BF16)
    z1_ref[...] = jnp.where(even, lower_out, upper_out).astype(BF16)
    copies[3].wait()


def spread_kernel(tiles, chunks, high_ref, low_ref, weight_ref, cell_ref, main_ref):
    main_ref[...] = jnp.zeros_like(main_ref)
    z_of_row = iota((CZ, 128), 0, jnp.int16)
    for t in range(tiles):
        parts = [], []
        for j in range(chunks):
            at = pl.ds(t * chunks + j, 1)
            z = z_weights(z_of_row, cell_ref[at, :], [weight_ref[c, at, :] for c in range(8)])
            for part, value in zip(parts, z):
                part.append(value)
        z_high, z_low = (jnp.concatenate(part, 1) for part in parts)
        s_high = high_ref[t * 4 * ROWS : (t + 1) * 4 * ROWS, :]
        s_low = low_ref[t * 4 * ROWS : (t + 1) * 4 * ROWS, :]
        both = nt_dot(jnp.concatenate([s_high, s_low], 0), z_high)
        got = both[: 4 * ROWS] + both[4 * ROWS :] + nt_dot(s_high, z_low)
        main_ref[t * ROWS : (t + 4) * ROWS, :] += got


def z_fold_kernel(tiles, group_planes, main_ref, z0_ref, z1_ref, got0_ref, got1_ref, out_ref, sent_ref):
    planes = tiles + EXT
    group = group_planes * ROWS
    units = []
    even = lax.rem(lax.axis_index("gz"), 2) == 0
    z0, z1, got0, got1 = (ref[...].astype(F32) for ref in (z0_ref, z1_ref, got0_ref, got1_ref))
    own_upper = jnp.where(even, z0, z1)
    own_lower = jnp.where(even, z1, z0)
    right_lower = jnp.where(even, got0, got1)
    left_upper = jnp.where(even, got1, got0)
    lane = iota((group, 128), 1)
    first = ((lane + LANES // 2) & (LANES - 1)) >= LANES // 2
    rim = (lane < LANES // 2) | (lane >= 128 - LANES // 2)
    halo = jnp.where(first, right_lower + own_upper, left_upper + own_lower)
    inner = jnp.where(first, left_upper, right_lower)
    for g in range(GROUPS):
        count = min(group, planes * ROWS - g * group)
        add = jnp.where(rim, pltpu.roll(inner, (-g * LANES) % 128, 1) if g else inner, 0.0)
        total = main_ref[g * group : g * group + count, :] + add[:count]
        out_ref[g * group : g * group + count, :] = total
        units += [total[at : at + ROWS] for at in range(0, count, ROWS)]
    out_ref[planes * ROWS : planes * ROWS + group, :] = halo
    units += [halo[at : at + ROWS] for at in range(0, group, ROWS)]
    inner = [unit[:CY] for unit in units]
    outer = [unit[CY:] for unit in units]
    outer = [
        pair[0] + pltpu.roll(pair[1], CY // 2, 0) if len(pair) > 1 else pair[0]
        for pair in (outer[u : u + 2] for u in range(0, len(outer), 2))
    ]
    halves = inner + outer
    halves += [jnp.zeros((CY, 128), F32)] * (len(halves) % 2)
    for u in range(0, len(halves), 2):
        sent_ref[u * CY : (u + 2) * CY, :] = jnp.concatenate(halves[u : u + 2], 0).astype(BF16)


def y_fold_kernel(n_gy, units, tiles, *refs):
    sources, (out_ref, far_ref, exact_ref) = refs[:n_gy], refs[n_gy:]
    half = iota((CY, 128), 0) < CY // 2
    filled = (iota((CY, 128), 0) < 2) | (iota((CY, 128), 0) == CY - 1)
    values = [ref[...].astype(F32) for ref in sources]
    wide = n_gy * CY
    planes = tiles + EXT
    for u in range(units):
        blocks = [None] * n_gy

        def add(b, value):
            b = b % n_gy
            blocks[b] = value if blocks[b] is None else blocks[b] + value

        for b, value in enumerate(values):
            if b == 0:
                first = value[u * ROWS : u * ROWS + CY]
                rest = value[u * ROWS + CY : (u + 1) * ROWS]
            else:
                first = value[u * CY : (u + 1) * CY]
                at = (units + u // 2) * CY
                rest = value[at : at + CY]
                rest = jnp.where(filled, pltpu.roll(rest, CY // 2, 0) if u % 2 else rest, 0.0)
            add(b, first)
            if n_gy == 2:
                add(b + 1, rest)
            else:
                add(b + 1, jnp.where(half, rest, 0.0))
                add(b - 1, jnp.where(half, 0.0, rest))
        exact = jnp.concatenate(blocks, 0)
        value = exact.astype(BF16)
        out_ref[u * wide : (u + 1) * wide, :] = value
        if u < EXT or planes - EXT <= u:
            v = u if u < EXT else u - planes + 2 * EXT
            far_ref[v * wide : (v + 1) * wide, :] = value
            exact_ref[v * wide : (v + 1) * wide, :] = exact


def along_z_taps(parts, row, radius):
    lane = iota((8, 128), 1)
    total = parts[radius, row : row + 8, :128]
    outside = [jnp.zeros((8, 128), F32)] * 3
    for k in range(2 * radius + 1):
        inner = parts[k, row : row + 8, :128]
        outer = parts[k, row : row + 8, 128:]
        step = radius - k
        if step:
            taken = lane >= 128 - step if step > 0 else lane < -step
            total = total + pltpu.roll(jnp.where(taken, outer, inner), step % 128, 1)
        for n, z in enumerate((-1, CZ, CZ + 1)):
            at = z - step
            value = inner if 0 <= at < CZ else outer
            outside[n] = jnp.where(lane == at % 128, value, outside[n])
    return total, [jnp.sum(v, axis=1, keepdims=True) for v in outside]


def rim_of(block, base, p, wide, group_planes):
    g, q = divmod(p, group_planes)
    packed = block[base + q * wide : base + (q + 1) * wide].astype(F32)
    return pltpu.roll(packed, (-g * LANES) % 128, 1) if g else packed


def own_kernel(tiles, group_planes, wide, span, own_ref, band_ref, total_ref, outside_ref, window, parts):
    planes = tiles + EXT
    radius = span // 2
    alone = tiles - EXT
    own = own_ref[...]
    lane = iota((wide, 128), 1)
    rim = (lane < LANES // 2) | (lane >= 128 - LANES // 2)
    for n in range(alone):
        rows = slice(n * wide, (n + 1) * wide)
        p = EXT + n
        window[rows, :128] = own[p * wide : (p + 1) * wide]
        edge = rim_of(own, planes * wide, p, wide, group_planes)
        window[rows, 128:] = jnp.where(rim, edge, 0.0).astype(BF16)
    for x in range(0, planes, AHEAD):
        first = (radius + EXT - x) * wide
        part = jnp.dot(
            band_ref[:, first : first + alone * wide], window[...], preferred_element_type=F32
        )
        at = row_of(x)
        for k in range(span):
            parts[k, at : at + STEP, :] = part[k * STEP : (k + 1) * STEP]
    lane = iota((8, 128), 1)
    for row in range(0, row_of(planes - 1) + TALL, 8):
        total, outside = along_z_taps(parts, row, radius)
        total_ref[row : row + 8, :] = total
        outside_ref[row : row + 8, :] = jnp.where(
            lane == 0, outside[0], jnp.where(lane == 1, outside[1], outside[2])
        )


def row_of(x):
    return x // AHEAD * STEP + x % AHEAD * TALL


def field_kernel(
    tiles, chunks, group_planes, wide, span,
    own_ref, got1_ref, got3_ref, lower_ref, upper_ref, band_ref, total_ref, outside_ref,
    hot_ref, weight_ref, z_ref, potential_ref, force_ref, window, parts, samples,
):
    planes = tiles + EXT
    radius = span // 2
    even = lax.rem(lax.axis_index("gx"), 2) == 0
    got1, got3 = got1_ref[...], got3_ref[...]
    right = jnp.where(even, got1, got3)
    left = jnp.where(even, got3, got1)
    own = own_ref[...]
    margin = planes * wide
    far_base = 2 * EXT * wide
    lane = iota((wide, 128), 1)
    rim = (lane < LANES // 2) | (lane >= 128 - LANES // 2)

    def main(block, p):
        return block[p * wide : (p + 1) * wide].astype(F32)

    def edge(block, p, base=margin):
        return rim_of(block, base, p, wide, group_planes)

    far_low, far_high = lower_ref[...], upper_ref[...]
    start, stop = radius + EXT, radius + tiles
    place = 0
    for x in range(2 * radius + planes):
        if start <= x < stop:
            continue
        terms = []
        if x < planes:
            terms.append((main(left, x), edge(left, x)))
        if 0 <= x - tiles < planes:
            p = x - tiles
            v = p if p < EXT else p - planes + 2 * EXT
            terms.append((main(own, v), edge(own, p, far_base)))
        if 0 <= x - 2 * tiles < planes:
            terms.append((main(right, x - 2 * tiles), edge(right, x - 2 * tiles)))
        if x < EXT:
            terms.append((main(far_low, EXT + x), edge(far_low, planes - EXT + x, far_base)))
        if 0 <= x - 3 * tiles < EXT:
            terms.append((main(far_high, x - 3 * tiles), edge(far_high, x - 3 * tiles, far_base)))
        rows = slice(place * wide, (place + 1) * wide)
        place += 1
        window[rows, :128] = sum(a for a, _ in terms).astype(BF16)
        window[rows, 128:] = jnp.where(
            rim, sum(b for _, b in terms), 0.0
        ).astype(BF16)

    for x in range(0, planes, AHEAD):
        count = min(AHEAD, planes - x)
        used = span + count - 1 - (stop - start)
        part = jnp.dot(
            band_ref[x // AHEAD, :, : used * wide],
            window[x * wide : (x + used) * wide, :],
            preferred_element_type=F32,
        )
        at = row_of(x)
        for k in range(span):
            parts[k, at : at + STEP, :] = part[k * STEP : (k + 1) * STEP]
    lane = iota((8, 128), 1)
    for row in range(0, row_of(planes - 1) + TALL, 8):
        total, outside = along_z_taps(parts, row, radius)
        total = total + total_ref[row : row + 8, :]
        below, above, beyond = (
            v + outside_ref[row : row + 8, n : n + 1] for n, v in enumerate(outside)
        )
        samples[0, row : row + 8, :] = jnp.where(lane == 0, below, pltpu.roll(total, 1, 1))
        samples[1, row : row + 8, :] = total
        samples[2, row : row + 8, :] = jnp.where(lane == CZ - 1, above, pltpu.roll(total, 127, 1))
        samples[3, row : row + 8, :] = jnp.where(
            lane == CZ - 1, beyond, jnp.where(lane == CZ - 2, above, pltpu.roll(total, 126, 1))
        )
    for x in range(tiles):
        potential_ref[x] = samples[1, row_of(x + 1) + 1 : row_of(x + 1) + 1 + CY, :]

    for t in range(tiles):
        rows = slice(row_of(t), row_of(t) + STEP)
        points = [samples[c, rows, :] for c in range(4)]
        points = points[:1] + [point - points[0] for point in points[1:]]
        halves = [jnp.concatenate(split(point), 1) for point in points]
        picked = jnp.dot(jnp.concatenate(halves, 0), hot_ref[t], preferred_element_type=F32)
        for j in range(chunks):
            at = t * chunks + j
            lanes = slice(j * 128, (j + 1) * 128)
            four = [picked[c * STEP : (c + 1) * STEP, lanes] for c in range(4)]
            value = four[0] + sum(z_ref[c, at : at + 1, :] * four[c] for c in range(1, 4))
            slope = sum(z_ref[4 + c, at : at + 1, :] * four[c] for c in range(1, 4))
            for d, part in enumerate((value, value, slope)):
                force_ref[d, at : at + 1, :] = jnp.sum(
                    weight_ref[t, d, :, lanes] * part, axis=0, keepdims=True
                )


def weight_kernel(tiles, chunks, charge_ref, offset_ref, cell_ref, hot_ref, weight_ref, z_ref, x_rows, y_rows):
    rows = tiles * chunks
    for r in range(0, rows, 8):
        at = pl.ds(r, 8)
        charge = charge_ref[at, :]
        xs = spline(offset_ref[at, :])
        ys = spline(offset_ref[pl.ds(rows + r, 8), :])
        zs = spline(offset_ref[pl.ds(2 * rows + r, 8), :])
        for w in range(2):
            for c in range(4):
                x_rows[4 * w + c, at, :] = -charge * xs[w][c]
                y_rows[4 * w + c, at, :] = ys[w][c]
                z_ref[4 * w + c, at, :] = zs[w][c]
    z_of_row = iota((CZ, 128), 0, jnp.int16)
    one, zero = jnp.ones((CZ, 128), BF16), jnp.zeros((CZ, 128), BF16)
    row = iota((STEP, 128), 0)
    for t in range(tiles):
        starts = [row_of(t + k) - row_of(t) for k in range(4)]
        plane = [row >= start for start in starts]
        y_of_row = row - sum(
            jnp.where(plane[k], starts[k] - starts[k - 1], 0) for k in range(1, 4)
        )
        for j in range(chunks):
            at = pl.ds(t * chunks + j, 1)
            lanes = slice(j * 128, (j + 1) * 128)
            cy = cell_ref[at, :] & (CY - 1)
            cz = cell_ref[pl.ds(rows + t * chunks + j, 1), :] & (CZ - 1)
            hot = jnp.where(z_of_row == tall(cz, jnp.int16, CZ), one, zero)
            hot_ref[t, :CZ, lanes] = hot
            hot_ref[t, CZ:, lanes] = hot
            gap = y_of_row - cy
            here = [gap == c for c in range(4)]

            def line(ref, n):
                return ref[n, at, :]

            y_value = y_slope = jnp.zeros((STEP, 128), F32)
            for c in range(4):
                y_value = jnp.where(here[c], line(y_rows, c), y_value)
                y_slope = jnp.where(here[c], line(y_rows, 4 + c), y_slope)
            x_value = x_slope = jnp.zeros((STEP, 128), F32)
            for k in range(4):
                x_value = jnp.where(plane[k], line(x_rows, k), x_value)
                x_slope = jnp.where(plane[k], line(x_rows, 4 + k), x_slope)
            weight_ref[t, 0, :, lanes] = x_slope * y_value
            weight_ref[t, 1, :, lanes] = x_value * y_slope
            weight_ref[t, 2, :, lanes] = x_value * y_value


def band_kernel(tiles, wide, kernel_ref, out_ref, other_ref, rows_ref):
    span = kernel_ref.shape[0]
    radius = span // 2
    columns = out_ref.shape[1]
    base = jnp.zeros((span, columns), F32)
    tap = iota((span, columns), 0)
    column = iota((span, columns), 1)
    for i in range(span):
        place = jnp.where(
            (column >= i * wide) & (column < (i + 1) * wide)
            & (((column - tap + radius) & (wide - 1)) == 0),
            1.0, 0.0,
        ).astype(BF16)
        base = base + lax.dot_general(
            kernel_ref[i], place, (((0,), (0,)), ((), ())), preferred_element_type=F32
        )
    rows_ref[...] = jnp.zeros_like(rows_ref)
    within = column & (wide - 1)
    for y in range(-1, CY + 2):
        shift = y % wide
        moved = base
        if shift:
            moved = jnp.where(
                within >= shift,
                pltpu.roll(base, shift, 1),
                pltpu.roll(base, (shift - wide) % columns, 1),
            )
        for n in range(AHEAD):
            there = pltpu.roll(moved, n * wide, 1) if n else moved
            for tile in range(columns // 128):
                at = pl.ds(n * TALL + y + 1, span, stride=STEP)
                rows_ref[tile, at, :] = there[:, tile * 128 : (tile + 1) * 128]
    alone = (tiles - EXT) * wide
    whole = jnp.concatenate([rows_ref[tile, : span * STEP] for tile in range(columns // 128)], 1)
    out_ref[...] = whole.astype(BF16)
    kept = other_ref.shape[2]
    moved = pltpu.roll(whole, columns - alone, 1)[:, :kept]
    lane = iota(moved.shape, 1)
    for n in range(other_ref.shape[0]):
        first = (radius + EXT - n * AHEAD) * wide
        other_ref[n] = jnp.where(lane < first, whole[:, :kept], moved).astype(BF16)


def vmem(n):
    return [pl.BlockSpec(memory_space=pltpu.VMEM)] * n


def local(charges, offsets, cells, kernel):
    n_gx, n_gy, n_gz = (lax.axis_size(axis) for axis in ("gx", "gy", "gz"))
    tiles, slots = charges.shape[0], charges.shape[3]
    span = kernel.shape[0]
    chunks = slots // 128
    rows = tiles * chunks
    planes = tiles + EXT
    group_planes = -(-planes // GROUPS)
    group = group_planes * ROWS
    wide = n_gy * CY
    band_columns = -(-(span + AHEAD - 1) * wide // 128) * 128
    charge = charges.reshape(rows, 128)
    offset = offsets.reshape(3 * rows, 128)
    cell = cells.reshape(2 * rows, 128)

    def shape(*dims, kind=F32):
        return jax.ShapeDtypeStruct(dims, kind)

    near = lambda n: [(i, i ^ 1) for i in range(n)]
    other = lambda n: [(i, (i + 1 if i % 2 else i - 1) % n) for i in range(n)]
    shift = lambda n, s: [(i, (i + s) % n) for i in range(n)]

    z0, z1, s_high, s_low, weights, z_cell, charge_in, offset_in, cell_in, kernel_in = pl.pallas_call(
        functools.partial(edge_kernel, tiles, chunks, group_planes),
        out_shape=(
            shape(group, 128, kind=BF16), shape(group, 128, kind=BF16),
            shape(tiles * 4 * ROWS, slots, kind=BF16), shape(tiles * 4 * ROWS, slots, kind=BF16),
            shape(8, rows, 128), shape(rows, 128, kind=jnp.int32),
            shape(rows, 128), shape(3 * rows, 128), shape(2 * rows, 128, kind=jnp.int32),
            shape(*kernel.shape, kind=kernel.dtype),
        ),
        in_specs=[pl.BlockSpec(memory_space=pltpu.HBM)] * 4,
        out_specs=tuple(vmem(10)),
        scratch_shapes=[
            pltpu.VMEM((4, rows, 128), F32),
            pltpu.VMEM((4, rows, 128), F32),
            pltpu.VMEM((GROUPS * group, 128), F32),
            pltpu.SemaphoreType.DMA((4,)),
        ],
        compiler_params=pltpu.CompilerParams(vmem_limit_bytes=8 << 20),
        name="edge",
    )(*(pltpu.with_memory_space_constraint(x, pltpu.HBM) for x in (charge, offset, cell, kernel)))
    got0 = lax.ppermute(z0, "gz", near(n_gz))
    got1 = lax.ppermute(z1, "gz", other(n_gz))
    main = pl.pallas_call(
        functools.partial(spread_kernel, tiles, chunks),
        out_shape=shape(planes * ROWS, 128),
        in_specs=vmem(4),
        out_specs=vmem(1)[0],
        compiler_params=pltpu.CompilerParams(vmem_limit_bytes=8 << 20),
        cost_estimate=pl.CostEstimate(flops=400_000_000, bytes_accessed=2_000_000, transcendentals=0),
        name="spread",
    )(s_high, s_low, weights, z_cell)
    units = planes + group_planes
    block, sent = pl.pallas_call(
        functools.partial(z_fold_kernel, tiles, group_planes),
        out_shape=(shape(units * ROWS, 128), shape(-(-(units + -(-units // 2)) // 2) * 2 * CY, 128, kind=BF16)),
        in_specs=vmem(5),
        out_specs=tuple(vmem(2)),
        compiler_params=pltpu.CompilerParams(vmem_limit_bytes=4 << 20),
        name="z_fold",
    )(main, z0, z1, got0, got1)
    sources = [block] + [lax.ppermute(sent, "gy", shift(n_gy, -s)) for s in range(1, n_gy)]
    mine, far, exact = pl.pallas_call(
        functools.partial(y_fold_kernel, n_gy, units, tiles),
        out_shape=(
            shape(units * wide, 128, kind=BF16),
            shape((2 * EXT + group_planes) * wide, 128, kind=BF16),
            shape((2 * EXT + group_planes) * wide, 128),
        ),
        in_specs=vmem(n_gy),
        out_specs=tuple(vmem(3)),
        compiler_params=pltpu.CompilerParams(vmem_limit_bytes=4 << 20),
        name="y_fold",
    )(*sources)
    x1 = lax.ppermute(mine, "gx", near(n_gx))
    lower = lax.ppermute(far, "gx", shift(n_gx, 2))
    upper = lower
    if n_gx != 4:
        upper = lax.ppermute(far, "gx", shift(n_gx, -2))
    x3 = lax.ppermute(mine, "gx", other(n_gx))
    other_columns = -(-(span + AHEAD - 1 - (tiles - EXT)) * wide // 128) * 128
    batches = -(-planes // AHEAD)
    band_call = pl.pallas_call(
        functools.partial(band_kernel, tiles, wide),
        out_shape=(
            shape(span * STEP, band_columns, kind=BF16),
            shape(batches, span * STEP, other_columns, kind=BF16),
        ),
        in_specs=vmem(1),
        out_specs=tuple(vmem(2)),
        scratch_shapes=[pltpu.VMEM((band_columns // 128, -(-span // 8) * 8 * STEP, 128), F32)],
        compiler_params=pltpu.CompilerParams(vmem_limit_bytes=16 << 20),
        cost_estimate=pl.CostEstimate(flops=400_000_000, bytes_accessed=2_000_000, transcendentals=0),
        name="band",
    )
    band, band_other = band_call(kernel_in)
    hot, weights_xy, weights_z = pl.pallas_call(
        functools.partial(weight_kernel, tiles, chunks),
        out_shape=(
            shape(tiles, 2 * CZ, slots, kind=BF16),
            shape(tiles, 3, STEP, slots),
            shape(8, rows, 128),
        ),
        in_specs=vmem(3),
        out_specs=tuple(vmem(3)),
        scratch_shapes=[pltpu.VMEM((8, rows, 128), F32), pltpu.VMEM((8, rows, 128), F32)],
        compiler_params=pltpu.CompilerParams(vmem_limit_bytes=12 << 20),
        cost_estimate=pl.CostEstimate(flops=400_000_000, bytes_accessed=2_000_000, transcendentals=0),
        name="weights",
    )(charge_in, offset_in, cell_in)
    own_total, own_outside = pl.pallas_call(
        functools.partial(own_kernel, tiles, group_planes, wide, span),
        out_shape=(shape(batches * STEP, 128), shape(batches * STEP, 128)),
        in_specs=vmem(2),
        out_specs=tuple(vmem(2)),
        scratch_shapes=[
            pltpu.VMEM(((tiles - EXT) * wide, 256), BF16),
            pltpu.VMEM((span, batches * STEP, 256), F32),
        ],
        compiler_params=pltpu.CompilerParams(vmem_limit_bytes=12 << 20),
        cost_estimate=pl.CostEstimate(flops=400_000_000, bytes_accessed=2_000_000, transcendentals=0),
        name="own",
    )(mine, band)
    potential, forces = pl.pallas_call(
        functools.partial(field_kernel, tiles, chunks, group_planes, wide, span),
        out_shape=(shape(tiles, CY, CZ), shape(3, rows, 128)),
        in_specs=vmem(11),
        out_specs=tuple(vmem(2)),
        scratch_shapes=[
            pltpu.VMEM(((2 * (span // 2) + planes) * wide, 256), BF16),
            pltpu.VMEM((span, -(-planes // AHEAD) * STEP, 256), F32),
            pltpu.VMEM((4, -(-planes // AHEAD) * STEP, 128), F32),
        ],
        compiler_params=pltpu.CompilerParams(vmem_limit_bytes=16 << 20),
        name="field",
    )(exact, x1, x3, lower, upper, band_other, own_total, own_outside, hot, weights_xy, weights_z)
    return potential, forces.reshape(3, tiles, 1, 1, slots)


def solution(mesh):
    placed = (
        P("gx", "gy", "gz", None),
        P(None, "gx", "gy", "gz", None),
        P(None, "gx", "gy", "gz", None),
        P(),
    )
    return jax.shard_map(
        local,
        mesh=mesh,
        in_specs=placed,
        out_specs=(P("gx", "gy", "gz"), P(None, "gx", "gy", "gz", None)),
        check_vma=False,
    )
```

```python
import functools

import jax
import jax.numpy as jnp
from jax import lax
from jax.experimental import pallas as pl
from jax.experimental.pallas import tpu as pltpu
from jax.sharding import PartitionSpec as P


CY = 8
CZ = 128
EXT = 3
ROWS = 16
TALL = CY + EXT
AHEAD = 4
STEP = -(-AHEAD * TALL // 8) * 8
LANES = 32
GROUPS = 128 // LANES

F32 = jnp.float32
BF16 = jnp.bfloat16


def spline(fraction):
    remain = 1.0 - fraction
    values = [
        remain**3 / 6.0,
        (3.0 * fraction**3 - 6.0 * fraction**2 + 4.0) / 6.0,
        (-3.0 * fraction**3 + 3.0 * fraction**2 + 3.0 * fraction + 1.0) / 6.0,
        fraction**3 / 6.0,
    ]
    slopes = [
        -0.5 * remain**2,
        1.5 * fraction**2 - 2.0 * fraction,
        -1.5 * fraction**2 + fraction + 0.5,
        0.5 * fraction**2,
    ]
    return values, slopes


def pick(distance, four):
    out = jnp.zeros((), F32)
    for c in reversed(range(4)):
        out = jnp.where(distance == c, four[c], out)
    return out


def split(x):
    high = x.astype(BF16)
    return high, (x - high.astype(F32)).astype(BF16)


def nt_dot(a, b):
    return lax.dot_general(a, b, (((1,), (1,)), ((), ())), preferred_element_type=F32)


def iota(shape, dim, kind=jnp.int32):
    return lax.broadcasted_iota(kind, shape, dim)


def tall(row, kind, count):
    tile = jnp.broadcast_to(row, (16, 128)).astype(kind)
    return jnp.concatenate([tile] * (count // 16), 0)


def z_weights(z_of_row, cell, rows):
    count = z_of_row.shape[0]
    high = low = jnp.zeros((count, 128), BF16)
    for c in range(4):
        here = z_of_row == tall(cell + (c - 1), jnp.int16, count)
        high = jnp.where(here, tall(rows[c], BF16, count), high)
        low = jnp.where(here, tall(rows[4 + c], BF16, count), low)
    return high, low


def edge_kernel(
    tiles, chunks, group_planes, charge_hbm, offset_hbm, cell_hbm, kernel_hbm,
    z0_ref, z1_ref, high_ref, low_ref, weight_ref, cell_ref,
    charge_in, offset_in, cell_in, kernel_in, x_rows, y_rows, acc, sems,
):
    copies = [
        pltpu.make_async_copy(source, target, sems.at[n])
        for n, (source, target) in enumerate(
            (
                (charge_hbm, charge_in),
                (offset_hbm, offset_in),
                (cell_hbm, cell_in),
                (kernel_hbm, kernel_in),
            )
        )
    ]
    for copy in copies:
        copy.start()
    rows = tiles * chunks
    acc[...] = jnp.zeros_like(acc)
    row = iota((LANES, 128), 0, jnp.int16)
    z_of_row = jnp.where(row < LANES // 2, row - 1, row + (CZ + 2 - LANES // 2 - 11))
    y_row = iota((ROWS, 128), 0)
    y_of_row = jnp.where(y_row < 12, y_row, y_row - ROWS)
    for copy in copies[:3]:
        copy.wait()
    for r in range(0, rows, 8):
        at = pl.ds(r, 8)
        xv, _ = spline(offset_in[at, :])
        yv, _ = spline(offset_in[pl.ds(rows + r, 8), :])
        zv, _ = spline(offset_in[pl.ds(2 * rows + r, 8), :])
        charge = charge_in[at, :]
        for c in range(4):
            x_rows[c, at, :] = charge * xv[c]
            y_rows[c, at, :] = yv[c]
            high = zv[c].astype(BF16).astype(F32)
            weight_ref[c, at, :] = high
            weight_ref[4 + c, at, :] = zv[c] - high
        cell_ref[at, :] = cell_in[pl.ds(rows + r, 8), :] & (CZ - 1)
    for t in range(tiles):
        parts = [], [], [], []
        for j in range(chunks):
            at = pl.ds(t * chunks + j, 1)
            cy = cell_in[at, :] & (CY - 1)
            y_dense = pick(y_of_row - (cy - 1), [y_rows[c, at, :] for c in range(4)])
            s = jnp.concatenate([y_dense * x_rows[k, at, :] for k in range(4)], 0)
            z = z_weights(z_of_row, cell_ref[at, :], [weight_ref[c, at, :] for c in range(8)])
            for part, value in zip(parts, split(s) + z):
                part.append(value)
        s_high, s_low, z_high, z_low = (jnp.concatenate(part, 1) for part in parts)
        high_ref[t * 4 * ROWS : (t + 1) * 4 * ROWS, :] = s_high
        low_ref[t * 4 * ROWS : (t + 1) * 4 * ROWS, :] = s_low
        both = nt_dot(jnp.concatenate([s_high, s_low], 0), z_high)
        got = both[: 4 * ROWS] + both[4 * ROWS :] + nt_dot(s_high, z_low)
        acc[t * ROWS : (t + 4) * ROWS, :LANES] += got
    group = group_planes * ROWS
    lane = iota((group, 128), 1)
    lower_out = jnp.zeros((group, 128), F32)
    upper_out = jnp.zeros((group, 128), F32)
    for g in range(GROUPS):
        edge = acc[g * group : (g + 1) * group, :]
        low = jnp.where(lane < LANES // 2, edge, 0.0)
        high = jnp.where(lane >= LANES // 2, edge, 0.0)
        lower_out = lower_out + pltpu.roll(low, (g * LANES - 1) % 128, 1)
        upper_out = upper_out + pltpu.roll(high, (g * LANES - LANES // 2 - 9) % 128, 1)
    even = lax.rem(lax.axis_index("gz"), 2) == 0
    z0_ref[...] = jnp.where(even, upper_out, lower_out).astype(BF16)
    z1_ref[...] = jnp.where(even, lower_out, upper_out).astype(BF16)
    copies[3].wait()


def spread_kernel(tiles, chunks, high_ref, low_ref, weight_ref, cell_ref, main_ref):
    main_ref[...] = jnp.zeros_like(main_ref)
    z_of_row = iota((CZ, 128), 0, jnp.int16)
    for t in range(tiles):
        parts = [], []
        for j in range(chunks):
            at = pl.ds(t * chunks + j, 1)
            z = z_weights(z_of_row, cell_ref[at, :], [weight_ref[c, at, :] for c in range(8)])
            for part, value in zip(parts, z):
                part.append(value)
        z_high, z_low = (jnp.concatenate(part, 1) for part in parts)
        s_high = high_ref[t * 4 * ROWS : (t + 1) * 4 * ROWS, :]
        s_low = low_ref[t * 4 * ROWS : (t + 1) * 4 * ROWS, :]
        both = nt_dot(jnp.concatenate([s_high, s_low], 0), z_high)
        got = both[: 4 * ROWS] + both[4 * ROWS :] + nt_dot(s_high, z_low)
        main_ref[t * ROWS : (t + 4) * ROWS, :] += got


def z_fold_kernel(tiles, group_planes, main_ref, z0_ref, z1_ref, got0_ref, got1_ref, out_ref, sent_ref):
    planes = tiles + EXT
    group = group_planes * ROWS
    units = []
    even = lax.rem(lax.axis_index("gz"), 2) == 0
    z0, z1, got0, got1 = (ref[...].astype(F32) for ref in (z0_ref, z1_ref, got0_ref, got1_ref))
    own_upper = jnp.where(even, z0, z1)
    own_lower = jnp.where(even, z1, z0)
    right_lower = jnp.where(even, got0, got1)
    left_upper = jnp.where(even, got1, got0)
    lane = iota((group, 128), 1)
    first = ((lane + LANES // 2) & (LANES - 1)) >= LANES // 2
    rim = (lane < LANES // 2) | (lane >= 128 - LANES // 2)
    halo = jnp.where(first, right_lower + own_upper, left_upper + own_lower)
    inner = jnp.where(first, left_upper, right_lower)
    for g in range(GROUPS):
        count = min(group, planes * ROWS - g * group)
        add = jnp.where(rim, pltpu.roll(inner, (-g * LANES) % 128, 1) if g else inner, 0.0)
        total = main_ref[g * group : g * group + count, :] + add[:count]
        out_ref[g * group : g * group + count, :] = total
        units += [total[at : at + ROWS] for at in range(0, count, ROWS)]
    out_ref[planes * ROWS : planes * ROWS + group, :] = halo
    units += [halo[at : at + ROWS] for at in range(0, group, ROWS)]
    inner = [unit[:CY] for unit in units]
    outer = [unit[CY:] for unit in units]
    outer = [
        pair[0] + pltpu.roll(pair[1], CY // 2, 0) if len(pair) > 1 else pair[0]
        for pair in (outer[u : u + 2] for u in range(0, len(outer), 2))
    ]
    halves = inner + outer
    halves += [jnp.zeros((CY, 128), F32)] * (len(halves) % 2)
    for u in range(0, len(halves), 2):
        sent_ref[u * CY : (u + 2) * CY, :] = jnp.concatenate(halves[u : u + 2], 0).astype(BF16)


def y_fold_kernel(n_gy, units, tiles, *refs):
    sources, (out_ref, far_ref, exact_ref) = refs[:n_gy], refs[n_gy:]
    half = iota((CY, 128), 0) < CY // 2
    filled = (iota((CY, 128), 0) < 2) | (iota((CY, 128), 0) == CY - 1)
    values = [ref[...].astype(F32) for ref in sources]
    wide = n_gy * CY
    planes = tiles + EXT
    for u in range(units):
        blocks = [None] * n_gy

        def add(b, value):
            b = b % n_gy
            blocks[b] = value if blocks[b] is None else blocks[b] + value

        for b, value in enumerate(values):
            if b == 0:
                first = value[u * ROWS : u * ROWS + CY]
                rest = value[u * ROWS + CY : (u + 1) * ROWS]
            else:
                first = value[u * CY : (u + 1) * CY]
                at = (units + u // 2) * CY
                rest = value[at : at + CY]
                rest = jnp.where(filled, pltpu.roll(rest, CY // 2, 0) if u % 2 else rest, 0.0)
            add(b, first)
            if n_gy == 2:
                add(b + 1, rest)
            else:
                add(b + 1, jnp.where(half, rest, 0.0))
                add(b - 1, jnp.where(half, 0.0, rest))
        exact = jnp.concatenate(blocks, 0)
        value = exact.astype(BF16)
        out_ref[u * wide : (u + 1) * wide, :] = value
        if u < EXT or planes - EXT <= u:
            v = u if u < EXT else u - planes + 2 * EXT
            far_ref[v * wide : (v + 1) * wide, :] = value
            exact_ref[v * wide : (v + 1) * wide, :] = exact


def along_z_taps(parts, row, radius):
    lane = iota((8, 128), 1)
    total = parts[radius, row : row + 8, :128]
    below = jnp.zeros((8, 128), F32)
    above = [jnp.zeros((8, 128), F32)] * 2
    for k in range(2 * radius + 1):
        inner = parts[k, row : row + 8, :128]
        outer = parts[k, row : row + 8, 128:]
        step = radius - k
        if step:
            taken = lane >= 128 - step if step > 0 else lane < -step
            total = total + pltpu.roll(jnp.where(taken, outer, inner), step % 128, 1)
        below = jnp.where(lane == (-1 - step) % 128, inner if step < 0 else outer, below)
        at, parity = CZ - step, step % 2
        if at == CZ - 1:
            above[parity] = jnp.where(lane == at, inner, jnp.where(lane == 0, outer, above[parity]))
        else:
            first = at % 128
            pair = (lane == first) | (lane == first + 1)
            above[parity] = jnp.where(pair, inner if at < CZ else outer, above[parity])
    even = (lane & 1) == 0
    outside = (below, jnp.where(even, above[0], above[1]), jnp.where(even, above[1], above[0]))
    return total, [jnp.sum(v, axis=1, keepdims=True) for v in outside]


def rim_of(block, base, p, wide, group_planes):
    g, q = divmod(p, group_planes)
    packed = block[base + q * wide : base + (q + 1) * wide].astype(F32)
    return pltpu.roll(packed, (-g * LANES) % 128, 1) if g else packed


def own_kernel(tiles, group_planes, wide, span, own_ref, band_ref, total_ref, outside_ref, window, parts):
    planes = tiles + EXT
    radius = span // 2
    alone = tiles - EXT
    own = own_ref[...]
    lane = iota((wide, 128), 1)
    rim = (lane < LANES // 2) | (lane >= 128 - LANES // 2)
    for n in range(alone):
        rows = slice(n * wide, (n + 1) * wide)
        p = EXT + n
        window[rows, :128] = own[p * wide : (p + 1) * wide]
        edge = rim_of(own, planes * wide, p, wide, group_planes)
        window[rows, 128:] = jnp.where(rim, edge, 0.0).astype(BF16)
    for x in range(0, planes, AHEAD):
        first = (radius + EXT - x) * wide
        part = jnp.dot(
            band_ref[:, first : first + alone * wide], window[...], preferred_element_type=F32
        )
        at = row_of(x)
        for k in range(span):
            parts[k, at : at + STEP, :] = part[k * STEP : (k + 1) * STEP]
    lane = iota((8, 128), 1)
    for row in range(0, row_of(planes - 1) + TALL, 8):
        total, outside = along_z_taps(parts, row, radius)
        total_ref[row : row + 8, :] = total
        outside_ref[row : row + 8, :] = jnp.where(
            lane == 0, outside[0], jnp.where(lane == 1, outside[1], outside[2])
        )


def row_of(x):
    return x // AHEAD * STEP + x % AHEAD * TALL


def field_kernel(
    tiles, chunks, group_planes, wide, span,
    own_ref, got1_ref, got3_ref, lower_ref, upper_ref, band_ref, total_ref, outside_ref,
    hot_ref, weight_ref, z_ref, potential_ref, force_ref, window, parts, samples,
):
    planes = tiles + EXT
    radius = span // 2
    even = lax.rem(lax.axis_index("gx"), 2) == 0
    got1, got3 = got1_ref[...], got3_ref[...]
    right = jnp.where(even, got1, got3)
    left = jnp.where(even, got3, got1)
    own = own_ref[...]
    margin = planes * wide
    far_base = 2 * EXT * wide
    lane = iota((wide, 128), 1)
    rim = (lane < LANES // 2) | (lane >= 128 - LANES // 2)

    def main(block, p):
        return block[p * wide : (p + 1) * wide].astype(F32)

    def edge(block, p, base=margin):
        return rim_of(block, base, p, wide, group_planes)

    far_low, far_high = lower_ref[...], upper_ref[...]
    start, stop = radius + EXT, radius + tiles
    place = 0
    for x in range(2 * radius + planes):
        if start <= x < stop:
            continue
        terms = []
        if x < planes:
            terms.append((main(left, x), edge(left, x)))
        if 0 <= x - tiles < planes:
            p = x - tiles
            v = p if p < EXT else p - planes + 2 * EXT
            terms.append((main(own, v), edge(own, p, far_base)))
        if 0 <= x - 2 * tiles < planes:
            terms.append((main(right, x - 2 * tiles), edge(right, x - 2 * tiles)))
        if x < EXT:
            terms.append((main(far_low, EXT + x), edge(far_low, planes - EXT + x, far_base)))
        if 0 <= x - 3 * tiles < EXT:
            terms.append((main(far_high, x - 3 * tiles), edge(far_high, x - 3 * tiles, far_base)))
        rows = slice(place * wide, (place + 1) * wide)
        place += 1
        window[rows, :128] = sum(a for a, _ in terms).astype(BF16)
        window[rows, 128:] = jnp.where(
            rim, sum(b for _, b in terms), 0.0
        ).astype(BF16)

    for x in range(0, planes, AHEAD):
        count = min(AHEAD, planes - x)
        used = span + count - 1 - (stop - start)
        part = jnp.dot(
            band_ref[x // AHEAD, :, : used * wide],
            window[x * wide : (x + used) * wide, :],
            preferred_element_type=F32,
        )
        at = row_of(x)
        for k in range(span):
            parts[k, at : at + STEP, :] = part[k * STEP : (k + 1) * STEP]
    lane = iota((8, 128), 1)
    for row in range(0, row_of(planes - 1) + TALL, 8):
        total, outside = along_z_taps(parts, row, radius)
        total = total + total_ref[row : row + 8, :]
        below, above, beyond = (
            v + outside_ref[row : row + 8, n : n + 1] for n, v in enumerate(outside)
        )
        samples[0, row : row + 8, :] = jnp.where(lane == 0, below, pltpu.roll(total, 1, 1))
        samples[1, row : row + 8, :] = total
        samples[2, row : row + 8, :] = jnp.where(lane == CZ - 1, above, pltpu.roll(total, 127, 1))
        samples[3, row : row + 8, :] = jnp.where(
            lane == CZ - 1, beyond, jnp.where(lane == CZ - 2, above, pltpu.roll(total, 126, 1))
        )
    for x in range(tiles):
        potential_ref[x] = samples[1, row_of(x + 1) + 1 : row_of(x + 1) + 1 + CY, :]

    for t in range(tiles):
        rows = slice(row_of(t), row_of(t) + STEP)
        points = [samples[c, rows, :] for c in range(4)]
        points = points[:1] + [point - points[0] for point in points[1:]]
        halves = [jnp.concatenate(split(point), 1) for point in points]
        picked = jnp.dot(jnp.concatenate(halves, 0), hot_ref[t], preferred_element_type=F32)
        for j in range(chunks):
            at = t * chunks + j
            lanes = slice(j * 128, (j + 1) * 128)
            four = [picked[c * STEP : (c + 1) * STEP, lanes] for c in range(4)]
            value = four[0] + sum(z_ref[c, at : at + 1, :] * four[c] for c in range(1, 4))
            slope = sum(z_ref[4 + c, at : at + 1, :] * four[c] for c in range(1, 4))
            for d, part in enumerate((value, value, slope)):
                force_ref[d, at : at + 1, :] = jnp.sum(
                    weight_ref[t, d, :, lanes] * part, axis=0, keepdims=True
                )


def weight_kernel(tiles, chunks, charge_ref, offset_ref, cell_ref, hot_ref, weight_ref, z_ref, x_rows, y_rows):
    rows = tiles * chunks
    for r in range(0, rows, 8):
        at = pl.ds(r, 8)
        charge = charge_ref[at, :]
        xs = spline(offset_ref[at, :])
        ys = spline(offset_ref[pl.ds(rows + r, 8), :])
        zs = spline(offset_ref[pl.ds(2 * rows + r, 8), :])
        for w in range(2):
            for c in range(4):
                x_rows[4 * w + c, at, :] = -charge * xs[w][c]
                y_rows[4 * w + c, at, :] = ys[w][c]
                z_ref[4 * w + c, at, :] = zs[w][c]
    z_of_row = iota((CZ, 128), 0, jnp.int16)
    one, zero = jnp.ones((CZ, 128), BF16), jnp.zeros((CZ, 128), BF16)
    row = iota((STEP, 128), 0)
    for t in range(tiles):
        starts = [row_of(t + k) - row_of(t) for k in range(4)]
        plane = [row >= start for start in starts]
        y_of_row = row - sum(
            jnp.where(plane[k], starts[k] - starts[k - 1], 0) for k in range(1, 4)
        )
        for j in range(chunks):
            at = pl.ds(t * chunks + j, 1)
            lanes = slice(j * 128, (j + 1) * 128)
            cy = cell_ref[at, :] & (CY - 1)
            cz = cell_ref[pl.ds(rows + t * chunks + j, 1), :] & (CZ - 1)
            hot = jnp.where(z_of_row == tall(cz, jnp.int16, CZ), one, zero)
            hot_ref[t, :CZ, lanes] = hot
            hot_ref[t, CZ:, lanes] = hot
            gap = y_of_row - cy
            here = [gap == c for c in range(4)]

            def line(ref, n):
                return ref[n, at, :]

            y_value = y_slope = jnp.zeros((STEP, 128), F32)
            for c in range(4):
                y_value = jnp.where(here[c], line(y_rows, c), y_value)
                y_slope = jnp.where(here[c], line(y_rows, 4 + c), y_slope)
            x_value = x_slope = jnp.zeros((STEP, 128), F32)
            for k in range(4):
                x_value = jnp.where(plane[k], line(x_rows, k), x_value)
                x_slope = jnp.where(plane[k], line(x_rows, 4 + k), x_slope)
            weight_ref[t, 0, :, lanes] = x_slope * y_value
            weight_ref[t, 1, :, lanes] = x_value * y_slope
            weight_ref[t, 2, :, lanes] = x_value * y_value


def band_kernel(tiles, wide, kernel_ref, out_ref, other_ref, rows_ref):
    span = kernel_ref.shape[0]
    radius = span // 2
    columns = out_ref.shape[1]
    base = jnp.zeros((span, columns), F32)
    tap = iota((span, columns), 0)
    column = iota((span, columns), 1)
    for i in range(span):
        place = jnp.where(
            (column >= i * wide) & (column < (i + 1) * wide)
            & (((column - tap + radius) & (wide - 1)) == 0),
            1.0, 0.0,
        ).astype(BF16)
        base = base + lax.dot_general(
            kernel_ref[i], place, (((0,), (0,)), ((), ())), preferred_element_type=F32
        )
    rows_ref[...] = jnp.zeros_like(rows_ref)
    within = column & (wide - 1)
    for y in range(-1, CY + 2):
        shift = y % wide
        moved = base
        if shift:
            moved = jnp.where(
                within >= shift,
                pltpu.roll(base, shift, 1),
                pltpu.roll(base, (shift - wide) % columns, 1),
            )
        for n in range(AHEAD):
            there = pltpu.roll(moved, n * wide, 1) if n else moved
            for tile in range(columns // 128):
                at = pl.ds(n * TALL + y + 1, span, stride=STEP)
                rows_ref[tile, at, :] = there[:, tile * 128 : (tile + 1) * 128]
    alone = (tiles - EXT) * wide
    whole = jnp.concatenate([rows_ref[tile, : span * STEP] for tile in range(columns // 128)], 1)
    out_ref[...] = whole.astype(BF16)
    kept = other_ref.shape[2]
    moved = pltpu.roll(whole, columns - alone, 1)[:, :kept]
    lane = iota(moved.shape, 1)
    for n in range(other_ref.shape[0]):
        first = (radius + EXT - n * AHEAD) * wide
        other_ref[n] = jnp.where(lane < first, whole[:, :kept], moved).astype(BF16)


def vmem(n):
    return [pl.BlockSpec(memory_space=pltpu.VMEM)] * n


def local(charges, offsets, cells, kernel):
    n_gx, n_gy, n_gz = (lax.axis_size(axis) for axis in ("gx", "gy", "gz"))
    tiles, slots = charges.shape[0], charges.shape[3]
    span = kernel.shape[0]
    chunks = slots // 128
    rows = tiles * chunks
    planes = tiles + EXT
    group_planes = -(-planes // GROUPS)
    group = group_planes * ROWS
    wide = n_gy * CY
    band_columns = -(-(span + AHEAD - 1) * wide // 128) * 128
    charge = charges.reshape(rows, 128)
    offset = offsets.reshape(3 * rows, 128)
    cell = cells.reshape(2 * rows, 128)

    def shape(*dims, kind=F32):
        return jax.ShapeDtypeStruct(dims, kind)

    near = lambda n: [(i, i ^ 1) for i in range(n)]
    other = lambda n: [(i, (i + 1 if i % 2 else i - 1) % n) for i in range(n)]
    shift = lambda n, s: [(i, (i + s) % n) for i in range(n)]

    z0, z1, s_high, s_low, weights, z_cell, charge_in, offset_in, cell_in, kernel_in = pl.pallas_call(
        functools.partial(edge_kernel, tiles, chunks, group_planes),
        out_shape=(
            shape(group, 128, kind=BF16), shape(group, 128, kind=BF16),
            shape(tiles * 4 * ROWS, slots, kind=BF16), shape(tiles * 4 * ROWS, slots, kind=BF16),
            shape(8, rows, 128), shape(rows, 128, kind=jnp.int32),
            shape(rows, 128), shape(3 * rows, 128), shape(2 * rows, 128, kind=jnp.int32),
            shape(*kernel.shape, kind=kernel.dtype),
        ),
        in_specs=[pl.BlockSpec(memory_space=pltpu.HBM)] * 4,
        out_specs=tuple(vmem(10)),
        scratch_shapes=[
            pltpu.VMEM((4, rows, 128), F32),
            pltpu.VMEM((4, rows, 128), F32),
            pltpu.VMEM((GROUPS * group, 128), F32),
            pltpu.SemaphoreType.DMA((4,)),
        ],
        compiler_params=pltpu.CompilerParams(vmem_limit_bytes=8 << 20),
        name="edge",
    )(*(pltpu.with_memory_space_constraint(x, pltpu.HBM) for x in (charge, offset, cell, kernel)))
    got0 = lax.ppermute(z0, "gz", near(n_gz))
    got1 = lax.ppermute(z1, "gz", other(n_gz))
    main = pl.pallas_call(
        functools.partial(spread_kernel, tiles, chunks),
        out_shape=shape(planes * ROWS, 128),
        in_specs=vmem(4),
        out_specs=vmem(1)[0],
        compiler_params=pltpu.CompilerParams(vmem_limit_bytes=8 << 20),
        cost_estimate=pl.CostEstimate(flops=400_000_000, bytes_accessed=2_000_000, transcendentals=0),
        name="spread",
    )(s_high, s_low, weights, z_cell)
    units = planes + group_planes
    block, sent = pl.pallas_call(
        functools.partial(z_fold_kernel, tiles, group_planes),
        out_shape=(shape(units * ROWS, 128), shape(-(-(units + -(-units // 2)) // 2) * 2 * CY, 128, kind=BF16)),
        in_specs=vmem(5),
        out_specs=tuple(vmem(2)),
        compiler_params=pltpu.CompilerParams(vmem_limit_bytes=4 << 20),
        name="z_fold",
    )(main, z0, z1, got0, got1)
    sources = [block] + [lax.ppermute(sent, "gy", shift(n_gy, -s)) for s in range(1, n_gy)]
    mine, far, exact = pl.pallas_call(
        functools.partial(y_fold_kernel, n_gy, units, tiles),
        out_shape=(
            shape(units * wide, 128, kind=BF16),
            shape((2 * EXT + group_planes) * wide, 128, kind=BF16),
            shape((2 * EXT + group_planes) * wide, 128),
        ),
        in_specs=vmem(n_gy),
        out_specs=tuple(vmem(3)),
        compiler_params=pltpu.CompilerParams(vmem_limit_bytes=4 << 20),
        name="y_fold",
    )(*sources)
    x1 = lax.ppermute(mine, "gx", near(n_gx))
    lower = lax.ppermute(far, "gx", shift(n_gx, 2))
    upper = lower
    if n_gx != 4:
        upper = lax.ppermute(far, "gx", shift(n_gx, -2))
    x3 = lax.ppermute(mine, "gx", other(n_gx))
    other_columns = -(-(span + AHEAD - 1 - (tiles - EXT)) * wide // 128) * 128
    batches = -(-planes // AHEAD)
    band_call = pl.pallas_call(
        functools.partial(band_kernel, tiles, wide),
        out_shape=(
            shape(span * STEP, band_columns, kind=BF16),
            shape(batches, span * STEP, other_columns, kind=BF16),
        ),
        in_specs=vmem(1),
        out_specs=tuple(vmem(2)),
        scratch_shapes=[pltpu.VMEM((band_columns // 128, -(-span // 8) * 8 * STEP, 128), F32)],
        compiler_params=pltpu.CompilerParams(vmem_limit_bytes=16 << 20),
        cost_estimate=pl.CostEstimate(flops=400_000_000, bytes_accessed=2_000_000, transcendentals=0),
        name="band",
    )
    band, band_other = band_call(kernel_in)
    hot, weights_xy, weights_z = pl.pallas_call(
        functools.partial(weight_kernel, tiles, chunks),
        out_shape=(
            shape(tiles, 2 * CZ, slots, kind=BF16),
            shape(tiles, 3, STEP, slots),
            shape(8, rows, 128),
        ),
        in_specs=vmem(3),
        out_specs=tuple(vmem(3)),
        scratch_shapes=[pltpu.VMEM((8, rows, 128), F32), pltpu.VMEM((8, rows, 128), F32)],
        compiler_params=pltpu.CompilerParams(vmem_limit_bytes=12 << 20),
        cost_estimate=pl.CostEstimate(flops=400_000_000, bytes_accessed=2_000_000, transcendentals=0),
        name="weights",
    )(charge_in, offset_in, cell_in)
    own_total, own_outside = pl.pallas_call(
        functools.partial(own_kernel, tiles, group_planes, wide, span),
        out_shape=(shape(batches * STEP, 128), shape(batches * STEP, 128)),
        in_specs=vmem(2),
        out_specs=tuple(vmem(2)),
        scratch_shapes=[
            pltpu.VMEM(((tiles - EXT) * wide, 256), BF16),
            pltpu.VMEM((span, batches * STEP, 256), F32),
        ],
        compiler_params=pltpu.CompilerParams(vmem_limit_bytes=12 << 20),
        cost_estimate=pl.CostEstimate(flops=400_000_000, bytes_accessed=2_000_000, transcendentals=0),
        name="own",
    )(mine, band)
    potential, forces = pl.pallas_call(
        functools.partial(field_kernel, tiles, chunks, group_planes, wide, span),
        out_shape=(shape(tiles, CY, CZ), shape(3, rows, 128)),
        in_specs=vmem(11),
        out_specs=tuple(vmem(2)),
        scratch_shapes=[
            pltpu.VMEM(((2 * (span // 2) + planes) * wide, 256), BF16),
            pltpu.VMEM((span, -(-planes // AHEAD) * STEP, 256), F32),
            pltpu.VMEM((4, -(-planes // AHEAD) * STEP, 128), F32),
        ],
        compiler_params=pltpu.CompilerParams(vmem_limit_bytes=16 << 20),
        name="field",
    )(exact, x1, x3, lower, upper, band_other, own_total, own_outside, hot, weights_xy, weights_z)
    return potential, forces.reshape(3, tiles, 1, 1, slots)


def solution(mesh):
    placed = (
        P("gx", "gy", "gz", None),
        P(None, "gx", "gy", "gz", None),
        P(None, "gx", "gy", "gz", None),
        P(),
    )
    return jax.shard_map(
        local,
        mesh=mesh,
        in_specs=placed,
        out_specs=(P("gx", "gy", "gz"), P(None, "gx", "gy", "gz", None)),
        check_vma=False,
    )
```
